32 devices in a mesh: light: 4 (over y, x), depth: 2 (over core), height: 4 (over z).
Axes of the slice: x: 2, y: 2, z: 4, core: 2. Of those that a mesh axis runs over, the one named last changes fastest.
Arguments:
- density: float32 [64, 32, 2048], P('light', 'depth', 'height'), may hold values from 0 to 6.4
- active_list: int32 [4, 48], P('depth'), may hold values from -1 to 63, as said below
- light_dir: int32 [8], replicated, may hold values from 0 to 1, as said below
- lamp_plane: float32 [8, 32, 2048], P(None, 'depth', 'height'), may hold values from 0.5 to 2
- extinction: float32 [8], replicated, may hold values from 0.015625 to 0.078125
- blur_weights: float32 [8, 25], replicated, may hold values from 0.2 to 16
- albedo: float32 [8], replicated, may hold values from 0.3 to 1
Outputs:
- rendered: float32 [8, 64, 2048], P('depth', 'light', 'height')
The draws below stay inside these ranges and needn't reach their ends.
Inputs may be any that keep to these rules, and one draw needn't show every extreme that they name: `active_list`: each row lists distinct brick numbers lb * 16 + hb (lb the light slab of 16 slices, hb the height brick of 128 cells) of one depth slab of 8 cells, then -1 to its end; a row lists between 24 and 48 bricks, and some row lists 48. `light_dir`: exactly 4 entries are 1.
All inputs are finite; a program needn't handle non-finite values.
Results may differ from the reference program's by a relative error of at most 0.00016.
Values sent between devices are 32-bit elements; how exact they have to be, the bound alone decides.
No kernel may reach another device: no remote copies, remote signals or barrier semaphores. Data moves between devices by JAX's collectives and lax.ppermute only.
A program may use at most 64 MiB of HBM per device.

```python
import math
import jax
import jax.numpy as jnp
from jax import lax

C = 8
LS = 16
BZ = 8
BH = 128
NL = 64
NZ = 32
NH = 2048
NHB = 16
NZB = 4
BRICKS = 64
SLOTS = 48


def draw_active_list(key, part):
    slab_keys = jax.random.split(jax.random.fold_in(key, 11), NZB)

    def one_slab(slab_key):
        shuffled = jax.random.permutation(slab_key, BRICKS).astype(jnp.int32)
        listed_count = jax.random.randint(jax.random.fold_in(slab_key, 3), (), SLOTS // 2, SLOTS + 1)
        return (shuffled[:SLOTS], listed_count)
    shuffled_rows, counts = jax.vmap(one_slab)(slab_keys)
    counts = counts.at[0].set(SLOTS)
    slot_index = jnp.arange(SLOTS, dtype=jnp.int32)
    return jnp.where(slot_index[None, :] < counts[:, None], shuffled_rows, -1).astype(jnp.int32)


def draw_light_dir(key, part):
    shuffled = jax.random.permutation(jax.random.fold_in(key, 7), C)
    return (shuffled >= C // 2).astype(jnp.int32)


def draw_density(key, part):
    slab_count = NL // LS
    low = jnp.log(jnp.float32(0.25))
    high = jnp.log(jnp.float32(2.0))
    along_height = jnp.exp(jax.random.uniform(jax.random.fold_in(key, 31), (slab_count, 1, NH), jnp.float32, low, high))
    along_depth = jnp.exp(jax.random.uniform(jax.random.fold_in(key, 32), (slab_count, NZ, 1), jnp.float32, low, high))
    cells = jax.random.uniform(jax.random.fold_in(key, 33), (slab_count, LS, NZ, NH), jnp.float32, 0.5, 1.5)
    factor = along_height * along_depth
    return (cells * factor[:, None]).reshape(NL, NZ, NH).astype(jnp.float32)


def draw_blur_weights(key, part):
    beside_all = jax.random.uniform(jax.random.fold_in(key, 41), (C, 25), jnp.float32, 0.2, 1.0)
    centre = jax.random.uniform(jax.random.fold_in(key, 42), (C,), jnp.float32, 8.0, 16.0)
    return beside_all.at[:, 12].set(centre).astype(jnp.float32)


def block_levels(key, dims, pieces, low, high):
    level, own = 1.0, jax.random.fold_in(key, 6)
    for dim, parts in pieces:
        steps = jnp.exp(jax.random.uniform(jax.random.fold_in(own, dim), (parts,), jnp.float32, low / len(pieces), high / len(pieces)))
        level = level * jnp.repeat(steps, dims[dim] // parts).reshape([-1 if axis == dim else 1 for axis in range(len(dims))])
    return level


def setup_inputs(seed: int = 0) -> dict:
    arg_keys = jax.random.split(jax.random.key(seed), 8)
    return {
        "density": draw_density(jax.random.fold_in(arg_keys[7], 71), 0),
        "active_list": draw_active_list(jax.random.fold_in(arg_keys[7], 71), 0),
        "light_dir": draw_light_dir(jax.random.fold_in(arg_keys[7], 71), 0),
        "lamp_plane": jnp.clip(0.5 + 1.5 * jax.random.uniform(arg_keys[3], (C, NZ, NH), jnp.float32) ** block_levels(arg_keys[3], (C, NZ, NH), ((1, 2), (2, 4)), -0.2, 0.2), 0.5, 2.0),
        "extinction": jnp.clip(jnp.exp(jax.random.uniform(arg_keys[4], (C,), jnp.float32, math.log(0.015625), math.log(0.078125))), 0.015625, 0.078125),
        "blur_weights": draw_blur_weights(jax.random.fold_in(arg_keys[7], 71), 0),
        "albedo": jnp.clip(jax.random.uniform(arg_keys[6], (C,), jnp.float32, 0.3, 1.0), 0.3, 1.0),
    }


def blur_plane(plane_in, kernel):
    depth_len = plane_in.shape[1]
    height_len = plane_in.shape[2]
    padded = jnp.pad(plane_in, ((0, 0), (2, 2), (2, 2)))
    total = jnp.zeros_like(plane_in)
    for row_off in range(5):
        for col_off in range(5):
            total = total + kernel[:, row_off, col_off, None, None] * padded[:, row_off:row_off + depth_len, col_off:col_off + height_len]
    return total


def live_cells(active_list):
    brick_ids = jnp.arange(BRICKS, dtype=jnp.int32)
    listed = jnp.any(active_list[:, :, None] == brick_ids[None, None, :], axis=1).astype(jnp.float32)
    listed = listed.reshape(NZB, NL // LS, NHB).transpose(1, 0, 2)
    return jnp.repeat(jnp.repeat(jnp.repeat(listed, LS, 0), BZ, 1), BH, 2)


def march(masked, lamp_plane, extinction, kernel, albedo):
    slabs = masked.reshape(NL // LS, LS, NZ, NH)

    def slab_step(plane_in, slab):
        before = jnp.cumsum(slab, axis=0) - slab

        def one_slice(packed):
            before_row, cells = packed
            lit = plane_in * jnp.exp(-extinction[:, None, None] * before_row[None])
            optical = 6.0 * cells / NZ
            depth_before = jnp.cumsum(optical, axis=0) - optical
            weight = jnp.exp(-depth_before) * (1.0 - jnp.exp(-optical))
            return jnp.sum(lit * weight[None], axis=1) * albedo[:, None]

        rows_out = lax.map(one_slice, (before, slab))
        leaving = plane_in * jnp.exp(-extinction[:, None, None] * jnp.sum(slab, axis=0)[None])
        return blur_plane(leaving, kernel), rows_out

    final_plane, rows_out = lax.scan(slab_step, lamp_plane, slabs)
    return rows_out.reshape(NL, C, NH).transpose(1, 0, 2)


def reference(density, active_list, light_dir, lamp_plane, extinction, blur_weights, albedo):
    kernel = (blur_weights / jnp.sum(blur_weights, axis=1, keepdims=True)).reshape(C, 5, 5)
    masked = density * live_cells(active_list)
    light_up = march(masked, lamp_plane, extinction, kernel, albedo)
    light_down = march(masked[::-1], lamp_plane, extinction, kernel, albedo)[:, ::-1, :]
    return jnp.where(light_dir[:, None, None] == 0, light_up, light_down)
```

```python
import jax
import jax.numpy as jnp
from jax import lax
from jax.experimental import pallas as pl
from jax.experimental.pallas import tpu as pltpu
from jax.sharding import PartitionSpec as P

BZ = 8
BH = 128
LANES = 128


def pairs_even(count):
    return [(i, i ^ 1) for i in range(count) if (i ^ 1) < count]


def pairs_odd(count):
    inner = [(i, i + 1) for i in range(1, count - 1, 2)]
    return inner + [(b, a) for a, b in inner]


def peer(position, k, count):
    if count & (count - 1) == 0:
        return position ^ k
    return (position - k) % count


def light_pairs(k, count):
    return [(peer(i, k, count), i) for i in range(count)]


def lane_iota(shape):
    return lax.broadcasted_iota(jnp.int32, shape, len(shape) - 1)


def slots(halo):
    return LANES // halo


def local(density, active_list, light_dir, lamp_plane, extinction, blur_weights, albedo):
    colours = extinction.shape[0]
    slices, depth_len, height_len = density.shape
    chain = lax.axis_size("light")
    groups = lax.axis_size("depth")
    columns = lax.axis_size("height")
    assert groups == 2
    mine = colours // groups
    full = depth_len * groups
    halo = 2 * (chain - 1)
    assert 2 * halo <= LANES
    wide = height_len + LANES
    per_tile = slots(halo)
    tiles = -(-(1 + colours) // per_tile)
    blocks = height_len // LANES
    slabs = depth_len // BZ

    def place(g):
        return g // per_tile, (g % per_tile) * halo

    def sums_kernel(density_ref, active_ref, lamp_ref, bundle_ref, column_ref, even_ref, odd_ref):
        light = lax.axis_index("light")
        depth = lax.axis_index("depth")
        height = lax.axis_index("height")
        listed = active_ref[...]
        first_brick = (light * columns + height) * blocks
        sums = []
        for j in range(blocks):
            hit = jnp.max(
                jnp.where(listed == first_brick + j, 1.0, 0.0), axis=1, keepdims=True
            )
            live = jnp.concatenate(
                [jnp.broadcast_to(hit[r : r + 1], (BZ, LANES)) for r in range(slabs)], axis=0
            )
            span = pl.ds(j * LANES, LANES)
            total = jnp.zeros((depth_len, LANES), jnp.float32)
            for x in range(slices):
                cell = density_ref[x, :, span] * live
                bundle_ref[x, :, span] = cell
                total = total + cell
            column_ref[:, span] = total
            sums.append(total)
        for i in range(mine):
            bundle_ref[slices + i] = lamp_ref[(1 - depth) * mine + i]
        lane = lane_iota((depth_len, LANES))
        low = [jnp.zeros((depth_len, LANES), jnp.float32) for _ in range(tiles)]
        high = [jnp.zeros((depth_len, LANES), jnp.float32) for _ in range(tiles)]
        for g in range(1 + colours):
            tile, shift = place(g)
            if g == 0:
                left, right = sums[0], sums[-1]
            else:
                owner = depth if g <= mine else 1 - depth
                c = owner * mine + (g - 1) % mine
                left = lamp_ref[c, :, pl.ds(0, LANES)]
                right = lamp_ref[c, :, pl.ds(height_len - LANES, LANES)]
            if shift:
                left = pltpu.roll(left, shift, 1)
                right = pltpu.roll(right, LANES - shift, 1)
            low[tile] = jnp.where((lane >= shift) & (lane < shift + halo), left, low[tile])
            high[tile] = jnp.where(
                (lane >= LANES - shift - halo) & (lane < LANES - shift), right, high[tile]
            )
        even_place = height % 2 == 0
        for t in range(tiles):
            span = pl.ds(t * LANES, LANES)
            even_ref[:, span] = jnp.where(even_place, high[t], low[t])
            odd_ref[:, span] = jnp.where(even_place, low[t], high[t])

    bundle, column, edge_even, edge_odd = pl.pallas_call(
        sums_kernel,
        name="sums",
        out_shape=(
            jax.ShapeDtypeStruct((slices + mine, depth_len, height_len), jnp.float32),
            jax.ShapeDtypeStruct((depth_len, height_len), jnp.float32),
            jax.ShapeDtypeStruct((depth_len, tiles * LANES), jnp.float32),
            jax.ShapeDtypeStruct((depth_len, tiles * LANES), jnp.float32),
        ),
    )(density, active_list, lamp_plane)

    got_even = lax.ppermute(edge_even, "height", pairs_even(columns))
    got_odd = lax.ppermute(edge_odd, "height", pairs_odd(columns))
    swap = [(0, 1), (1, 0)]
    theirs = lax.ppermute(bundle, "depth", swap)

    def widen_kernel(column_ref, even_ref, odd_ref, wide_ref, halos_ref):
        even_place = lax.axis_index("height") % 2 == 0
        lane = lane_iota((depth_len, LANES))
        for t in range(tiles):
            span = pl.ds(t * LANES, LANES)
            a, b = even_ref[:, span], odd_ref[:, span]
            from_right = jnp.where(even_place, a, b)
            from_left = jnp.where(even_place, b, a)
            halos_ref[:, span] = from_right
            halos_ref[:, pl.ds((tiles + t) * LANES, LANES)] = from_left
            if t == 0:
                edge = jnp.where(
                    lane < halo, from_right, jnp.where(lane >= LANES - halo, from_left, 0.0)
                )
                wide_ref[:, pl.ds(height_len, LANES)] = edge
        wide_ref[:, pl.ds(0, height_len)] = column_ref[...]

    wide_column, halos = pl.pallas_call(
        widen_kernel,
        name="widen",
        out_shape=(
            jax.ShapeDtypeStruct((depth_len, wide), jnp.float32),
            jax.ShapeDtypeStruct((depth_len, 2 * tiles * LANES), jnp.float32),
        ),
    )(column, got_even, got_odd)

    near = [lax.ppermute(wide_column, "light", light_pairs(k, chain)) for k in range(1, chain)]
    far_halos = lax.ppermute(halos, "depth", swap)
    far = [lax.ppermute(block, "depth", swap) for block in near]

    def gains_kernel(dir_ref, ext_ref, own_ref, other_ref, gain_ref, cells):
        depth = lax.axis_index("depth")
        for x in range(slices):
            row = pl.multiple_of(x * full + depth * depth_len, BZ)
            cells[pl.ds(row, depth_len), :] = own_ref[x]
            row = pl.multiple_of(x * full + (1 - depth) * depth_len, BZ)
            cells[pl.ds(row, depth_len), :] = other_ref[x]
        rows = lax.broadcasted_iota(jnp.int32, (slices, LANES), 0)
        down = [dir_ref[depth * mine + i] == 1 for i in range(mine)]
        rate = [ext_ref[depth * mine + i] for i in range(mine)]

        def one_depth(z, through):
            cell = cells[pl.ds(z, slices, stride=full), :]
            running = cell
            step = 1
            while step < slices:
                running = running + jnp.where(
                    rows >= step, pltpu.roll(running, step, 0), 0.0
                )
                step *= 2
            before_up = running - cell
            before_down = running[slices - 1 : slices] - running
            kept = jnp.exp(-(6.0 * cell / full))
            weight = through * (1.0 - kept)
            for i in range(mine):
                before = jnp.where(down[i], before_down, before_up)
                gain_ref[i, z] = weight * jnp.exp(-rate[i] * before)
            return through * kept

        lax.fori_loop(0, full, one_depth, jnp.ones((slices, LANES), jnp.float32))

    gains = pl.pallas_call(
        gains_kernel,
        name="gains",
        grid=(blocks,),
        in_specs=[
            pl.BlockSpec(memory_space=pltpu.SMEM),
            pl.BlockSpec(memory_space=pltpu.SMEM),
            pl.BlockSpec((slices, depth_len, LANES), lambda j: (0, 0, j)),
            pl.BlockSpec((slices, depth_len, LANES), lambda j: (0, 0, j)),
        ],
        out_specs=pl.BlockSpec((mine, full, slices, LANES), lambda j: (0, 0, 0, j)),
        out_shape=jax.ShapeDtypeStruct((mine, full, slices, height_len), jnp.float32),
        scratch_shapes=[pltpu.VMEM((slices * full, LANES), jnp.float32)],
    )(light_dir, extinction, bundle, theirs)

    def chain_kernel(
        dir_ref, ext_ref, blur_ref, albedo_ref, lamp_ref, theirs_ref, halos_ref, far_halos_ref,
        *rest,
    ):
        near_refs = rest[: chain - 1]
        far_refs = rest[chain - 1 : 2 * (chain - 1)]
        gain_hbm, out_ref, gain, lamp_far, walls, plane, dimmed, arrivals = rest[2 * (chain - 1) :]
        fetch_lamp = pltpu.make_async_copy(
            theirs_ref.at[pl.ds(slices, mine)], lamp_far, arrivals.at[0]
        )
        fetch_lamp.start()
        fetch_gain = pltpu.make_async_copy(gain_hbm, gain, arrivals.at[1])
        fetch_gain.start()
        light = lax.axis_index("light")
        depth = lax.axis_index("depth")
        height = lax.axis_index("height")
        own_row = pl.multiple_of(depth * depth_len, BZ)
        other_row = pl.multiple_of((1 - depth) * depth_len, BZ)
        for k in range(1, chain):
            source = peer(light, k, chain)
            walls[source, pl.ds(own_row, depth_len), :] = near_refs[k - 1][...]
            walls[source, pl.ds(other_row, depth_len), :] = far_refs[k - 1][...]
        lane = lane_iota((depth_len, LANES))
        fetch_lamp.wait()
        for i in range(mine):
            for row, group, edges, body in (
                (own_row, 1 + i, halos_ref, lamp_ref[depth * mine + i]),
                (other_row, 1 + mine + i, far_halos_ref, lamp_far[i]),
            ):
                tile, shift = place(group)
                from_right = edges[:, pl.ds(tile * LANES, LANES)]
                from_left = edges[:, pl.ds((tiles + tile) * LANES, LANES)]
                if shift:
                    from_right = pltpu.roll(from_right, LANES - shift, 1)
                    from_left = pltpu.roll(from_left, shift, 1)
                edge = jnp.where(
                    lane < halo, from_right, jnp.where(lane >= LANES - halo, from_left, 0.0)
                )
                plane[i, pl.ds(row, depth_len), pl.ds(0, height_len)] = body
                plane[i, pl.ds(row, depth_len), pl.ds(height_len, LANES)] = edge
        margin = jnp.zeros((BZ, wide), jnp.float32)
        dimmed[pl.ds(0, BZ), :] = margin
        dimmed[pl.ds(BZ + full, BZ), :] = margin
        wide_lane = lane_iota((BZ, wide))
        inside = (
            (wide_lane < height_len)
            | ((wide_lane < height_len + LANES // 2) & (height < columns - 1))
            | ((wide_lane >= height_len + LANES // 2) & (height > 0))
        )

        for i in range(mine):
            c = depth * mine + i
            goes_down = dir_ref[c] == 1
            steps = jnp.where(goes_down, chain - 1 - light, light)
            norm = blur_ref[c, 0]
            for tap in range(1, 25):
                norm = norm + blur_ref[c, tap]
            scale = jnp.where(inside, 1.0 / jnp.full((BZ, wide), norm, jnp.float32), 0.0)
            rate = ext_ref[c]

            def one_step(s, carry):
                source = jnp.where(goes_down, chain - 1 - s, s)
                for r in range(full // BZ):
                    span = pl.ds(r * BZ, BZ)
                    dimmed[pl.ds(BZ + r * BZ, BZ), :] = (
                        plane[i, span, :] * jnp.exp(-rate * walls[source, span, :]) * scale
                    )
                for r in range(full // BZ):
                    shifted = [dimmed[pl.ds(BZ + r * BZ + a - 2, BZ), :] for a in range(5)]
                    total = None
                    for b in range(5):
                        part = blur_ref[c, b] * shifted[0]
                        for a in range(1, 5):
                            part = part + blur_ref[c, a * 5 + b] * shifted[a]
                        if b != 2:
                            part = pltpu.roll(part, (2 - b) % wide, 1)
                        total = part if total is None else total + part
                    plane[i, pl.ds(r * BZ, BZ), :] = total
                return carry

            lax.fori_loop(0, steps, one_step, 0)
        fetch_gain.wait()
        for i in range(mine):
            shade = albedo_ref[depth * mine + i]
            for j in range(blocks):
                span = pl.ds(j * LANES, LANES)
                parts = [jnp.zeros((slices, LANES), jnp.float32) for _ in range(4)]
                for z in range(full):
                    row = plane[i, pl.ds(z, 1), span]
                    parts[z % 4] = parts[z % 4] + row * gain[i, z, :, span]
                out_ref[i, :, span] = shade * ((parts[0] + parts[1]) + (parts[2] + parts[3]))

    smem = pl.BlockSpec(memory_space=pltpu.SMEM)
    vmem = pl.BlockSpec(memory_space=pltpu.VMEM)
    return pl.pallas_call(
        chain_kernel,
        name="chain",
        in_specs=[smem] * 4
        + [
            vmem,
            pl.BlockSpec(memory_space=pl.ANY),
            vmem,
            vmem,
        ]
        + [vmem] * (2 * (chain - 1))
        + [pl.BlockSpec(memory_space=pl.ANY)],
        out_specs=vmem,
        out_shape=jax.ShapeDtypeStruct((mine, slices, height_len), jnp.float32),
        scratch_shapes=[
            pltpu.VMEM((mine, full, slices, height_len), jnp.float32),
            pltpu.VMEM((mine, depth_len, height_len), jnp.float32),
            pltpu.VMEM((chain, full, wide), jnp.float32),
            pltpu.VMEM((mine, full, wide), jnp.float32),
            pltpu.VMEM((full + 2 * BZ, wide), jnp.float32),
            pltpu.SemaphoreType.DMA((2,)),
        ],
    )(
        light_dir, extinction, blur_weights, albedo, lamp_plane, theirs, halos, far_halos,
        *near, *far, gains,
    )


def solution(mesh):
    in_specs = (
        P("light", "depth", "height"),
        P("depth", None),
        P(),
        P(None, "depth", "height"),
        P(),
        P(),
        P(),
    )
    out_specs = P("depth", "light", "height")
    return jax.shard_map(local, mesh=mesh, in_specs=in_specs, out_specs=out_specs, check_vma=False)
```

```python
import jax
import jax.numpy as jnp
from jax import lax
from jax.experimental import pallas as pl
from jax.experimental.pallas import tpu as pltpu
from jax.sharding import PartitionSpec as P

BZ = 8
BH = 128
LANES = 128
GRANT = pltpu.CompilerParams(vmem_limit_bytes=24 << 20)


def pairs_even(count):
    return [(i, i ^ 1) for i in range(count) if (i ^ 1) < count]


def pairs_odd(count):
    inner = [(i, i + 1) for i in range(1, count - 1, 2)]
    return inner + [(b, a) for a, b in inner]


def peer(position, k, count):
    if count & (count - 1) == 0:
        return position ^ k
    return (position - k) % count


def light_pairs(k, count):
    return [(peer(i, k, count), i) for i in range(count)]


def lane_iota(shape):
    return lax.broadcasted_iota(jnp.int32, shape, len(shape) - 1)


def near_memory(value):
    return pltpu.with_memory_space_constraint(value, pltpu.VMEM)


def slots(halo):
    return LANES // halo


def local(density, active_list, light_dir, lamp_plane, extinction, blur_weights, albedo):
    colours = extinction.shape[0]
    slices, depth_len, height_len = density.shape
    chain = lax.axis_size("light")
    groups = lax.axis_size("depth")
    columns = lax.axis_size("height")
    assert groups == 2
    mine = colours // groups
    full = depth_len * groups
    halo = 2 * (chain - 1)
    assert 2 * halo <= LANES
    wide = height_len + LANES
    per_tile = slots(halo)
    tiles = -(-(1 + colours) // per_tile)
    blocks = height_len // LANES
    slabs = depth_len // BZ

    def place(g):
        return g // per_tile, (g % per_tile) * halo

    def sums_kernel(density_ref, active_ref, lamp_ref, bundle_ref, column_ref, even_ref, odd_ref):
        light = lax.axis_index("light")
        depth = lax.axis_index("depth")
        height = lax.axis_index("height")
        listed = active_ref[...]
        first_brick = (light * columns + height) * blocks
        sums = []
        for j in range(blocks):
            hit = jnp.max(
                jnp.where(listed == first_brick + j, 1.0, 0.0), axis=1, keepdims=True
            )
            live = jnp.concatenate(
                [jnp.broadcast_to(hit[r : r + 1], (BZ, LANES)) for r in range(slabs)], axis=0
            )
            span = pl.ds(j * LANES, LANES)
            total = jnp.zeros((depth_len, LANES), jnp.float32)
            for x in range(slices):
                cell = density_ref[x, :, span] * live
                bundle_ref[x, :, span] = cell
                total = total + cell
            column_ref[:, span] = total
            sums.append(total)
        for i in range(mine):
            bundle_ref[slices + i] = lamp_ref[(1 - depth) * mine + i]
        lane = lane_iota((depth_len, LANES))
        low = [jnp.zeros((depth_len, LANES), jnp.float32) for _ in range(tiles)]
        high = [jnp.zeros((depth_len, LANES), jnp.float32) for _ in range(tiles)]
        for g in range(1 + colours):
            tile, shift = place(g)
            if g == 0:
                left, right = sums[0], sums[-1]
            else:
                owner = depth if g <= mine else 1 - depth
                c = owner * mine + (g - 1) % mine
                left = lamp_ref[c, :, pl.ds(0, LANES)]
                right = lamp_ref[c, :, pl.ds(height_len - LANES, LANES)]
            if shift:
                left = pltpu.roll(left, shift, 1)
                right = pltpu.roll(right, LANES - shift, 1)
            low[tile] = jnp.where((lane >= shift) & (lane < shift + halo), left, low[tile])
            high[tile] = jnp.where(
                (lane >= LANES - shift - halo) & (lane < LANES - shift), right, high[tile]
            )
        even_place = height % 2 == 0
        for t in range(tiles):
            span = pl.ds(t * LANES, LANES)
            even_ref[:, span] = jnp.where(even_place, high[t], low[t])
            odd_ref[:, span] = jnp.where(even_place, low[t], high[t])

    bundle, column, edge_even, edge_odd = pl.pallas_call(
        sums_kernel,
        name="sums",
        compiler_params=GRANT,
        out_shape=(
            pltpu.VMEM((slices + mine, depth_len, height_len), jnp.float32),
            pltpu.VMEM((depth_len, height_len), jnp.float32),
            pltpu.VMEM((depth_len, tiles * LANES), jnp.float32),
            pltpu.VMEM((depth_len, tiles * LANES), jnp.float32),
        ),
    )(density, active_list, lamp_plane)

    got_even = lax.ppermute(edge_even, "height", pairs_even(columns))
    got_odd = lax.ppermute(edge_odd, "height", pairs_odd(columns))
    swap = [(0, 1), (1, 0)]
    theirs = lax.ppermute(bundle, "depth", swap)

    def widen_kernel(column_ref, even_ref, odd_ref, wide_ref, halos_ref):
        even_place = lax.axis_index("height") % 2 == 0
        lane = lane_iota((depth_len, LANES))
        for t in range(tiles):
            span = pl.ds(t * LANES, LANES)
            a, b = even_ref[:, span], odd_ref[:, span]
            from_right = jnp.where(even_place, a, b)
            from_left = jnp.where(even_place, b, a)
            halos_ref[:, span] = from_right
            halos_ref[:, pl.ds((tiles + t) * LANES, LANES)] = from_left
            if t == 0:
                edge = jnp.where(
                    lane < halo, from_right, jnp.where(lane >= LANES - halo, from_left, 0.0)
                )
                wide_ref[:, pl.ds(height_len, LANES)] = edge
        wide_ref[:, pl.ds(0, height_len)] = column_ref[...]

    wide_column, halos = pl.pallas_call(
        widen_kernel,
        name="widen",
        compiler_params=GRANT,
        out_shape=(
            pltpu.VMEM((depth_len, wide), jnp.float32),
            pltpu.VMEM((depth_len, 2 * tiles * LANES), jnp.float32),
        ),
    )(near_memory(column), near_memory(got_even), near_memory(got_odd))

    near = [lax.ppermute(wide_column, "light", light_pairs(k, chain)) for k in range(1, chain)]
    far_halos = lax.ppermute(halos, "depth", swap)
    far = [lax.ppermute(block, "depth", swap) for block in near]

    def gains_kernel(dir_ref, ext_ref, own_ref, other_ref, gain_ref, cells, earlier):
        depth = lax.axis_index("depth")
        for ref, half in ((own_ref, depth), (other_ref, 1 - depth)):
            for j in range(blocks):
                span = pl.ds(j * LANES, LANES)
                running = jnp.zeros((depth_len, LANES), jnp.float32)
                for x in range(slices):
                    row = pl.multiple_of(x * full + half * depth_len, BZ)
                    cell = ref[x, :, span]
                    cells[j, pl.ds(row, depth_len), :] = cell
                    earlier[j, pl.ds(row, depth_len), :] = running
                    running = running + cell
                row = pl.multiple_of(slices * full + half * depth_len, BZ)
                earlier[j, pl.ds(row, depth_len), :] = running
        down = [dir_ref[depth * mine + i] == 1 for i in range(mine)]
        rate = [-ext_ref[depth * mine + i] for i in range(mine)]

        def one_depth(z, through):
            passed = []
            for j in range(blocks):
                span = pl.ds(j * LANES, LANES)
                cell = cells[j, pl.ds(z, slices, stride=full), :]
                before_up = earlier[j, pl.ds(z, slices, stride=full), :]
                total = earlier[j, pl.ds(slices * full + z, 1), :]
                before_down = total - before_up - cell
                kept = jnp.exp(cell * (-6.0 / full))
                weight = through[j] * (1.0 - kept)
                for i in range(mine):
                    before = jnp.where(down[i], before_down, before_up)
                    gain_ref[i, z, :, span] = weight * jnp.exp(rate[i] * before)
                passed.append(through[j] * kept)
            return tuple(passed)

        lax.fori_loop(
            0, full, one_depth, tuple(jnp.ones((slices, LANES), jnp.float32) for _ in range(blocks))
        )

    smem = pl.BlockSpec(memory_space=pltpu.SMEM)
    vmem = pl.BlockSpec(memory_space=pltpu.VMEM)
    gains = pl.pallas_call(
        gains_kernel,
        name="gains",
        compiler_params=GRANT,
        in_specs=[smem, smem, vmem, vmem],
        out_shape=pltpu.VMEM((mine, full, slices, height_len), jnp.float32),
        scratch_shapes=[
            pltpu.VMEM((blocks, slices * full, LANES), jnp.float32),
            pltpu.VMEM((blocks, (slices + 1) * full, LANES), jnp.float32),
        ],
    )(light_dir, extinction, near_memory(bundle), near_memory(theirs))

    def chain_kernel(
        dir_ref, ext_ref, blur_ref, albedo_ref, lamp_ref, theirs_ref, halos_ref, far_halos_ref,
        *rest,
    ):
        near_refs = rest[: chain - 1]
        far_refs = rest[chain - 1 : 2 * (chain - 1)]
        gain, out_ref, walls, plane, dimmed = rest[2 * (chain - 1) :]
        light = lax.axis_index("light")
        depth = lax.axis_index("depth")
        height = lax.axis_index("height")
        own_row = pl.multiple_of(depth * depth_len, BZ)
        other_row = pl.multiple_of((1 - depth) * depth_len, BZ)
        for k in range(1, chain):
            source = peer(light, k, chain)
            walls[source, pl.ds(own_row, depth_len), :] = near_refs[k - 1][...]
            walls[source, pl.ds(other_row, depth_len), :] = far_refs[k - 1][...]
        lane = lane_iota((depth_len, LANES))
        for i in range(mine):
            for row, group, edges, body in (
                (own_row, 1 + i, halos_ref, lamp_ref[depth * mine + i]),
                (other_row, 1 + mine + i, far_halos_ref, theirs_ref[slices + i]),
            ):
                tile, shift = place(group)
                from_right = edges[:, pl.ds(tile * LANES, LANES)]
                from_left = edges[:, pl.ds((tiles + tile) * LANES, LANES)]
                if shift:
                    from_right = pltpu.roll(from_right, LANES - shift, 1)
                    from_left = pltpu.roll(from_left, shift, 1)
                edge = jnp.where(
                    lane < halo, from_right, jnp.where(lane >= LANES - halo, from_left, 0.0)
                )
                plane[i, pl.ds(row, depth_len), pl.ds(0, height_len)] = body
                plane[i, pl.ds(row, depth_len), pl.ds(height_len, LANES)] = edge
        margin = jnp.zeros((BZ, wide), jnp.float32)
        dimmed[pl.ds(0, BZ), :] = margin
        dimmed[pl.ds(BZ + full, BZ), :] = margin
        wide_lane = lane_iota((BZ, wide))
        inside = (
            (wide_lane < height_len)
            | ((wide_lane < height_len + LANES // 2) & (height < columns - 1))
            | ((wide_lane >= height_len + LANES // 2) & (height > 0))
        )

        for i in range(mine):
            c = depth * mine + i
            goes_down = dir_ref[c] == 1
            steps = jnp.where(goes_down, chain - 1 - light, light)
            norm = blur_ref[c, 0]
            for tap in range(1, 25):
                norm = norm + blur_ref[c, tap]
            scale = jnp.where(inside, 1.0 / jnp.full((BZ, wide), norm, jnp.float32), 0.0)
            rate = ext_ref[c]

            def one_step(s, carry):
                source = jnp.where(goes_down, chain - 1 - s, s)
                for r in range(full // BZ):
                    span = pl.ds(r * BZ, BZ)
                    dimmed[pl.ds(BZ + r * BZ, BZ), :] = (
                        plane[i, span, :] * jnp.exp(-rate * walls[source, span, :]) * scale
                    )
                for r in range(full // BZ):
                    shifted = [dimmed[pl.ds(BZ + r * BZ + a - 2, BZ), :] for a in range(5)]
                    total = None
                    for b in range(5):
                        part = blur_ref[c, b] * shifted[0]
                        for a in range(1, 5):
                            part = part + blur_ref[c, a * 5 + b] * shifted[a]
                        if b != 2:
                            part = pltpu.roll(part, (2 - b) % wide, 1)
                        total = part if total is None else total + part
                    plane[i, pl.ds(r * BZ, BZ), :] = total
                return carry

            lax.fori_loop(0, steps, one_step, 0)
        for i in range(mine):
            shade = albedo_ref[depth * mine + i]
            for j in range(blocks):
                span = pl.ds(j * LANES, LANES)
                parts = [jnp.zeros((slices, LANES), jnp.float32) for _ in range(4)]
                for z in range(full):
                    row = plane[i, pl.ds(z, 1), span]
                    parts[z % 4] = parts[z % 4] + row * gain[i, z, :, span]
                out_ref[i, :, span] = shade * ((parts[0] + parts[1]) + (parts[2] + parts[3]))

    return pl.pallas_call(
        chain_kernel,
        name="chain",
        compiler_params=GRANT,
        in_specs=[smem] * 4 + [vmem] * (4 + 2 * (chain - 1) + 1),
        out_specs=vmem,
        out_shape=jax.ShapeDtypeStruct((mine, slices, height_len), jnp.float32),
        scratch_shapes=[
            pltpu.VMEM((chain, full, wide), jnp.float32),
            pltpu.VMEM((mine, full, wide), jnp.float32),
            pltpu.VMEM((full + 2 * BZ, wide), jnp.float32),
        ],
    )(
        light_dir, extinction, blur_weights, albedo, lamp_plane,
        *[near_memory(v) for v in (theirs, halos, far_halos, *near, *far, gains)],
    )


def solution(mesh):
    in_specs = (
        P("light", "depth", "height"),
        P("depth", None),
        P(),
        P(None, "depth", "height"),
        P(),
        P(),
        P(),
    )
    out_specs = P("depth", "light", "height")
    return jax.shard_map(local, mesh=mesh, in_specs=in_specs, out_specs=out_specs, check_vma=False)
```

```python
import jax
import jax.numpy as jnp
from jax import lax
from jax.experimental import pallas as pl
from jax.experimental.pallas import tpu as pltpu
from jax.sharding import PartitionSpec as P

BZ = 8
LANES = 128
TAPS = 5
GRANT = pltpu.CompilerParams(vmem_limit_bytes=24 << 20)
SMEM = pl.BlockSpec(memory_space=pltpu.SMEM)
VMEM = pl.BlockSpec(memory_space=pltpu.VMEM)
HBM = pl.BlockSpec(memory_space=pltpu.HBM)


def pairs_even(count):
    return [(i, i ^ 1) for i in range(count) if (i ^ 1) < count]


def pairs_odd(count):
    inner = [(i, i + 1) for i in range(1, count - 1, 2)]
    return inner + [(b, a) for a, b in inner]


def peer(position, k, count):
    if count & (count - 1) == 0:
        return position ^ k
    return (position - k) % count


def light_pairs(k, count):
    return [(peer(i, k, count), i) for i in range(count)]


def lane_iota(shape):
    return lax.broadcasted_iota(jnp.int32, shape, len(shape) - 1)


def in_vmem(*values):
    return [pltpu.with_memory_space_constraint(v, pltpu.VMEM) for v in values]


def in_hbm(*values):
    return [pltpu.with_memory_space_constraint(v, pltpu.HBM) for v in values]


def in_smem(*values):
    return [pltpu.with_memory_space_constraint(v, pltpu.SMEM) for v in values]


def split(value):
    high = value.astype(jnp.bfloat16)
    return high, (value - high.astype(jnp.float32)).astype(jnp.bfloat16)


def local(density, active_list, light_dir, lamp_plane, extinction, blur_weights, albedo):
    colours = extinction.shape[0]
    slices, depth_len, height_len = density.shape
    chain = lax.axis_size("light")
    groups = lax.axis_size("depth")
    columns = lax.axis_size("height")
    assert groups == 2
    mine = colours // groups
    full = depth_len * groups
    halo = 2 * (chain - 1)
    assert 2 * halo <= LANES
    wide = height_len + LANES
    per_tile = LANES // halo
    tiles = -(-(1 + colours) // per_tile)
    assert 2 * tiles * LANES <= wide * chain
    blocks = height_len // LANES
    slabs = depth_len // BZ
    halo_rows = -(-2 * tiles * LANES // wide) * depth_len

    def place(g):
        return g // per_tile, (g % per_tile) * halo

    def sums_kernel(
        density_hbm, active_hbm, lamp_hbm, dir_hbm, ext_hbm, blur_hbm, albedo_hbm,
        bundle_ref, column_ref, even_ref, odd_ref, dir_ref, ext_ref, blur_ref, albedo_ref,
        density_ref, active_ref, lamp_ref, arrivals,
    ):
        light = lax.axis_index("light")
        depth = lax.axis_index("depth")
        height = lax.axis_index("height")
        moves = [
            pltpu.make_async_copy(source, target, arrivals.at[i])
            for i, (source, target) in enumerate(
                (
                    (density_hbm, density_ref),
                    (active_hbm, active_ref),
                    (lamp_hbm, lamp_ref),
                    (lamp_hbm.at[pl.ds((1 - depth) * mine, mine)], bundle_ref.at[pl.ds(slices, mine)]),
                    (dir_hbm, dir_ref),
                    (ext_hbm, ext_ref),
                    (blur_hbm, blur_ref),
                    (albedo_hbm, albedo_ref),
                )
            )
        ]
        for move in moves:
            move.start()
        moves[1].wait()
        listed = active_ref[...]
        first_brick = (light * columns + height) * blocks
        hits = [
            jnp.max(jnp.where(listed == first_brick + j, 1.0, 0.0), axis=1, keepdims=True)
            for j in range(blocks)
        ]
        moves[0].wait()
        sums = []
        for j, hit in enumerate(hits):
            live = jnp.concatenate(
                [jnp.broadcast_to(hit[r : r + 1], (BZ, LANES)) for r in range(slabs)], axis=0
            )
            span = pl.ds(j * LANES, LANES)
            total = jnp.zeros((depth_len, LANES), jnp.float32)
            for x in range(slices):
                cell = density_ref[x, :, span] * live
                bundle_ref[x, :, span] = cell
                total = total + cell
            column_ref[:, span] = total
            sums.append(total)
        moves[2].wait()
        lane = lane_iota((depth_len, LANES))
        low = [jnp.zeros((depth_len, LANES), jnp.float32) for _ in range(tiles)]
        high = [jnp.zeros((depth_len, LANES), jnp.float32) for _ in range(tiles)]
        for g in range(1 + colours):
            tile, shift = place(g)
            if g == 0:
                left, right = sums[0], sums[-1]
            else:
                owner = depth if g <= mine else 1 - depth
                c = owner * mine + (g - 1) % mine
                left = lamp_ref[c, :, pl.ds(0, LANES)]
                right = lamp_ref[c, :, pl.ds(height_len - LANES, LANES)]
            if shift:
                left = pltpu.roll(left, shift, 1)
                right = pltpu.roll(right, LANES - shift, 1)
            low[tile] = jnp.where((lane >= shift) & (lane < shift + halo), left, low[tile])
            high[tile] = jnp.where(
                (lane >= LANES - shift - halo) & (lane < LANES - shift), right, high[tile]
            )
        even_place = height % 2 == 0
        for t in range(tiles):
            span = pl.ds(t * LANES, LANES)
            even_ref[:, span] = jnp.where(even_place, high[t], low[t])
            odd_ref[:, span] = jnp.where(even_place, low[t], high[t])
        for move in moves[3:]:
            move.wait()

    bundle, column, edge_even, edge_odd, dirs, exts, blurs, albedos = pl.pallas_call(
        sums_kernel,
        name="sums",
        compiler_params=GRANT,
        in_specs=[HBM] * 7,
        out_specs=[VMEM] * 4 + [SMEM] * 4,
        out_shape=(
            pltpu.VMEM((slices + mine, depth_len, height_len), jnp.float32),
            pltpu.VMEM((depth_len, height_len), jnp.float32),
            pltpu.VMEM((depth_len, tiles * LANES), jnp.float32),
            pltpu.VMEM((depth_len, tiles * LANES), jnp.float32),
            pltpu.SMEM(light_dir.shape, jnp.int32),
            pltpu.SMEM(extinction.shape, jnp.float32),
            pltpu.SMEM(blur_weights.shape, jnp.float32),
            pltpu.SMEM(albedo.shape, jnp.float32),
        ),
        scratch_shapes=[
            pltpu.VMEM(density.shape, jnp.float32),
            pltpu.VMEM(active_list.shape, jnp.int32),
            pltpu.VMEM(lamp_plane.shape, jnp.float32),
            pltpu.SemaphoreType.DMA((8,)),
        ],
    )(*in_hbm(density, active_list, lamp_plane, light_dir, extinction, blur_weights, albedo))

    swap = [(0, 1), (1, 0)]
    theirs = lax.ppermute(bundle, "depth", swap)
    got_even = lax.ppermute(edge_even, "height", pairs_even(columns))
    got_odd = lax.ppermute(edge_odd, "height", pairs_odd(columns))

    def gains_body(dir_ref, ext_ref, cells_ref, gain_ref, through_ref, cells, earlier):
        depth = lax.axis_index("depth")
        for j in range(blocks):
            running = jnp.zeros((depth_len, LANES), jnp.float32)
            for x in range(slices):
                rows = pl.ds(x * depth_len, depth_len)
                cell = cells_ref[x, :, pl.ds(j * LANES, LANES)]
                cells[j, rows, :] = cell
                earlier[j, rows, :] = running
                running = running + cell
            earlier[j, pl.ds(slices * depth_len, depth_len), :] = running
        down = [dir_ref[depth * mine + i] == 1 for i in range(mine)]
        rate = [-ext_ref[depth * mine + i] for i in range(mine)]

        def one_depth(z, through):
            passed = []
            for j in range(blocks):
                span = pl.ds(j * LANES, LANES)
                cell = cells[j, pl.ds(z, slices, stride=depth_len), :]
                before_up = earlier[j, pl.ds(z, slices, stride=depth_len), :]
                total = earlier[j, pl.ds(slices * depth_len + z, 1), :]
                before_down = total - before_up - cell
                kept = jnp.exp(cell * (-6.0 / full))
                weight = through[j] * (1.0 - kept)
                for i in range(mine):
                    before = jnp.where(down[i], before_down, before_up)
                    gain_ref[i, z, :, span] = weight * jnp.exp(rate[i] * before)
                passed.append(through[j] * kept)
            return tuple(passed)

        start = tuple(jnp.ones((slices, LANES), jnp.float32) for _ in range(blocks))
        for j, value in enumerate(lax.fori_loop(0, depth_len, one_depth, start)):
            through_ref[:, pl.ds(j * LANES, LANES)] = value

    gains_shape = (
        pltpu.VMEM((mine, depth_len, slices, height_len), jnp.float32),
        pltpu.VMEM((slices, height_len), jnp.float32),
    )
    gains_scratch = [
        pltpu.VMEM((blocks, slices * depth_len, LANES), jnp.float32),
        pltpu.VMEM((blocks, (slices + 1) * depth_len, LANES), jnp.float32),
    ]

    def near_kernel(dir_ref, ext_ref, blur_ref, cells_ref, gain_ref, through_ref, taps_ref, *scratch):
        depth = lax.axis_index("depth")
        shape = (full, LANES)
        lane = lane_iota(shape)
        offset = lane % full - lax.broadcasted_iota(jnp.int32, shape, 0) + TAPS // 2
        for i in range(mine):
            c = depth * mine + i
            norm = blur_ref[c, 0]
            for tap in range(1, TAPS * TAPS):
                norm = norm + blur_ref[c, tap]
            inverse = 1.0 / jnp.full(shape, norm, jnp.float32)
            for b in range(TAPS):
                band = jnp.zeros(shape, jnp.float32)
                for a in range(TAPS):
                    band = jnp.where(offset == a, blur_ref[c, a * TAPS + b], band)
                band = band * inverse
                high = band.astype(jnp.bfloat16).astype(jnp.float32)
                band = jnp.where(lane < 2 * full, high, band - high)
                taps_ref[i, pl.ds(b * full, full), :] = band.astype(jnp.bfloat16)[:, : 3 * full]
        gains_body(dir_ref, ext_ref, cells_ref, gain_ref, through_ref, *scratch)

    gain_near, through_near, taps = pl.pallas_call(
        near_kernel,
        name="near_gains",
        compiler_params=GRANT,
        in_specs=[SMEM] * 3 + [VMEM],
        out_shape=gains_shape + (pltpu.VMEM((mine, TAPS * full, 3 * full), jnp.bfloat16),),
        scratch_shapes=gains_scratch,
    )(*in_smem(dirs, exts, blurs), *in_vmem(bundle))

    def widen_kernel(column_ref, even_ref, odd_ref, wide_ref, halos_ref):
        even_place = lax.axis_index("height") % 2 == 0
        lane = lane_iota((depth_len, LANES))
        for t in range(tiles):
            span = pl.ds(t * LANES, LANES)
            a, b = even_ref[:, span], odd_ref[:, span]
            from_right = jnp.where(even_place, a, b)
            from_left = jnp.where(even_place, b, a)
            halos_ref[:, span] = from_right
            halos_ref[:, pl.ds((tiles + t) * LANES, LANES)] = from_left
            if t == 0:
                edge = jnp.where(
                    lane < halo, from_right, jnp.where(lane >= LANES - halo, from_left, 0.0)
                )
                wide_ref[:, pl.ds(height_len, LANES)] = edge
        wide_ref[:, pl.ds(0, height_len)] = column_ref[...]

    wide_column, halos = pl.pallas_call(
        widen_kernel,
        name="widen",
        compiler_params=GRANT,
        out_shape=(
            pltpu.VMEM((depth_len, wide), jnp.float32),
            pltpu.VMEM((depth_len, 2 * tiles * LANES), jnp.float32),
        ),
    )(*in_vmem(column, got_even, got_odd))

    near = []
    for k in range(1, chain):
        near.append(lax.ppermute(wide_column, "light", light_pairs(k, chain)))

    gain_far, through_far = pl.pallas_call(
        gains_body,
        name="far_gains",
        compiler_params=GRANT,
        in_specs=[SMEM] * 2 + [VMEM],
        out_shape=gains_shape,
        scratch_shapes=gains_scratch,
    )(*in_smem(dirs, exts), *in_vmem(theirs))

    def join_kernel(*refs):
        out_ref = refs[-1]
        for k, ref in enumerate(refs[: chain - 1]):
            out_ref[pl.ds(k * depth_len, depth_len), :] = ref[...]
        for t in range(2 * tiles):
            row, lane = divmod(t * LANES, wide)
            out_ref[pl.ds((chain - 1 + row) * depth_len, depth_len), pl.ds(lane, LANES)] = refs[
                chain - 1
            ][:, pl.ds(t * LANES, LANES)]

    parcel = pl.pallas_call(
        join_kernel,
        name="join",
        compiler_params=GRANT,
        out_shape=pltpu.VMEM(((chain - 1) * depth_len + halo_rows, wide), jnp.float32),
    )(*in_vmem(*near, halos))
    far = lax.ppermute(parcel, "depth", swap)

    def chain_kernel(
        dir_ref, ext_ref, albedo_ref, lamp_ref, theirs_ref, near_ref, far_ref, taps_ref,
        gain_near_ref, through_near_ref, gain_far_ref, through_far_ref, out_ref, walls, plane, lit,
    ):
        light = lax.axis_index("light")
        depth = lax.axis_index("depth")
        height = lax.axis_index("height")
        own_row = pl.multiple_of(depth * depth_len, BZ)
        other_row = pl.multiple_of((1 - depth) * depth_len, BZ)
        for k in range(1, chain):
            source = peer(light, k, chain)
            rows = pl.ds((k - 1) * depth_len, depth_len)
            walls[source, pl.ds(own_row, depth_len), :] = near_ref[rows, :]
            walls[source, pl.ds(other_row, depth_len), :] = far_ref[rows, :]
        lane = lane_iota((depth_len, LANES))

        def halo_tile(ref, t):
            row, first = divmod(t * LANES, wide)
            return ref[pl.ds((chain - 1 + row) * depth_len, depth_len), pl.ds(first, LANES)]

        for i in range(mine):
            for row, group, edges, body in (
                (own_row, 1 + i, near_ref, lamp_ref[depth * mine + i]),
                (other_row, 1 + mine + i, far_ref, theirs_ref[slices + i]),
            ):
                tile, shift = place(group)
                from_right = halo_tile(edges, tile)
                from_left = halo_tile(edges, tiles + tile)
                if shift:
                    from_right = pltpu.roll(from_right, LANES - shift, 1)
                    from_left = pltpu.roll(from_left, shift, 1)
                edge = jnp.where(
                    lane < halo, from_right, jnp.where(lane >= LANES - halo, from_left, 0.0)
                )
                plane[i, pl.ds(row, depth_len), pl.ds(0, height_len)] = body
                plane[i, pl.ds(row, depth_len), pl.ds(height_len, LANES)] = edge
        wide_lane = lane_iota((1, wide))
        inside = (
            (wide_lane < height_len)
            | ((wide_lane < height_len + LANES // 2) & (height < columns - 1))
            | ((wide_lane >= height_len + LANES // 2) & (height > 0))
        )
        inside = jnp.where(inside, 1.0, 0.0)
        down = [dir_ref[depth * mine + i] == 1 for i in range(mine)]
        steps = [jnp.where(d, chain - 1 - light, light) for d in down]
        rate = [-ext_ref[depth * mine + i] for i in range(mine)]

        def one_step(s, carry):
            for i in range(mine):
                wall = walls[jnp.where(down[i], chain - 1 - s, s)]
                before = plane[i]
                high, low = split(before * (jnp.exp(rate[i] * wall) * inside))
                bands = jnp.dot(
                    taps_ref[i],
                    jnp.concatenate([high, low, high], axis=0),
                    preferred_element_type=jnp.float32,
                )
                after = None
                for b in range(TAPS):
                    part = bands[b * full : (b + 1) * full]
                    if b != TAPS // 2:
                        part = pltpu.roll(part, (TAPS // 2 - b) % wide, 1)
                    after = part if after is None else after + part
                plane[i] = jnp.where(s < steps[i], after, before)
            return carry

        lax.fori_loop(0, jnp.maximum(light, chain - 1 - light), one_step, 0)
        in_front = depth == 0
        for i in range(mine):
            for half, row in enumerate((own_row, other_row)):
                lit[half, i] = plane[i, pl.ds(row, depth_len), pl.ds(0, height_len)]
            shade = albedo_ref[depth * mine + i]
            for j in range(blocks):
                span = pl.ds(j * LANES, LANES)
                sums = []
                for half, gain in enumerate((gain_near_ref, gain_far_ref)):
                    parts = [jnp.zeros((slices, LANES), jnp.float32) for _ in range(2)]
                    for z in range(depth_len):
                        light_row = lit[half, i, pl.ds(z, 1), span]
                        parts[z % 2] = parts[z % 2] + light_row * gain[i, z, :, span]
                    sums.append(parts[0] + parts[1])
                front = jnp.where(in_front, sums[0], sums[1])
                back = jnp.where(in_front, sums[1], sums[0])
                through = jnp.where(in_front, through_near_ref[:, span], through_far_ref[:, span])
                out_ref[i, :, span] = shade * (front + through * back)

    return pl.pallas_call(
        chain_kernel,
        name="chain",
        compiler_params=GRANT,
        in_specs=[SMEM] * 3 + [VMEM] * 9,
        out_specs=VMEM,
        out_shape=jax.ShapeDtypeStruct((mine, slices, height_len), jnp.float32),
        scratch_shapes=[
            pltpu.VMEM((chain, full, wide), jnp.float32),
            pltpu.VMEM((mine, full, wide), jnp.float32),
            pltpu.VMEM((groups, mine, depth_len, height_len), jnp.float32),
        ],
    )(
        *in_smem(dirs, exts, albedos),
        *in_vmem(lamp_plane, theirs, parcel, far, taps),
        *in_vmem(gain_near, through_near, gain_far, through_far),
    )


def solution(mesh):
    in_specs = (
        P("light", "depth", "height"),
        P("depth", None),
        P(),
        P(None, "depth", "height"),
        P(),
        P(),
        P(),
    )
    out_specs = P("depth", "light", "height")

    return jax.shard_map(local, mesh=mesh, in_specs=in_specs, out_specs=out_specs, check_vma=False)
```

```python
import jax
import jax.numpy as jnp
from jax import lax
from jax.experimental import pallas as pl
from jax.experimental.pallas import tpu as pltpu
from jax.sharding import PartitionSpec as P

BZ = 8
LANES = 128
TAPS = 5
GRANT = pltpu.CompilerParams(vmem_limit_bytes=24 << 20)
SMEM = pl.BlockSpec(memory_space=pltpu.SMEM)
VMEM = pl.BlockSpec(memory_space=pltpu.VMEM)
HBM = pl.BlockSpec(memory_space=pltpu.HBM)


def swaps(first, count):
    pairs = {i: i for i in range(count)}
    for i in range(first, count - 1, 2):
        pairs[i], pairs[i + 1] = i + 1, i
    return sorted(pairs.items())


def peer(position, k, count):
    if count & (count - 1) == 0:
        return position ^ k
    return (position - k) % count


def light_pairs(k, count):
    return [(peer(i, k, count), i) for i in range(count)]


def lane_iota(shape):
    return lax.broadcasted_iota(jnp.int32, shape, len(shape) - 1)


def in_vmem(*values):
    return [pltpu.with_memory_space_constraint(v, pltpu.VMEM) for v in values]


def in_hbm(*values):
    return [pltpu.with_memory_space_constraint(v, pltpu.HBM) for v in values]


def in_smem(*values):
    return [pltpu.with_memory_space_constraint(v, pltpu.SMEM) for v in values]


def split(value):
    high = value.astype(jnp.bfloat16)
    return high, (value - high.astype(jnp.float32)).astype(jnp.bfloat16)


def local(density, active_list, light_dir, lamp_plane, extinction, blur_weights, albedo):
    colours = extinction.shape[0]
    slices, depth_len, height_len = density.shape
    chain = lax.axis_size("light")
    groups = lax.axis_size("depth")
    columns = lax.axis_size("height")
    assert groups == 2
    mine = colours // groups
    full = depth_len * groups
    halo = 2 * (chain - 1)
    assert 2 * halo <= LANES
    wide = height_len + LANES
    per_tile = LANES // halo
    tiles = -(-(1 + colours) // per_tile)
    assert 2 * tiles * LANES <= wide * chain
    blocks = height_len // LANES
    slabs = depth_len // BZ
    halo_rows = -(-2 * tiles * LANES // wide) * depth_len

    def place(g):
        return g // per_tile, (g % per_tile) * halo

    def sums_kernel(
        density_hbm, active_hbm, lamp_hbm, dir_hbm, ext_hbm, blur_hbm, albedo_hbm,
        bundle_ref, column_ref, even_ref, odd_ref, dir_ref, ext_ref, blur_ref, albedo_ref,
        density_ref, active_ref, lamp_ref, arrivals,
    ):
        light = lax.axis_index("light")
        depth = lax.axis_index("depth")
        height = lax.axis_index("height")
        moves = [
            pltpu.make_async_copy(source, target, arrivals.at[i])
            for i, (source, target) in enumerate(
                (
                    (density_hbm, density_ref),
                    (active_hbm, active_ref),
                    (lamp_hbm, lamp_ref),
                    (lamp_hbm.at[pl.ds((1 - depth) * mine, mine)], bundle_ref.at[pl.ds(slices, mine)]),
                    (dir_hbm, dir_ref),
                    (ext_hbm, ext_ref),
                    (blur_hbm, blur_ref),
                    (albedo_hbm, albedo_ref),
                )
            )
        ]
        for move in moves:
            move.start()
        moves[1].wait()
        listed = active_ref[...]
        first_brick = (light * columns + height) * blocks
        hits = [
            jnp.max(jnp.where(listed == first_brick + j, 1.0, 0.0), axis=1, keepdims=True)
            for j in range(blocks)
        ]
        moves[0].wait()
        sums = []
        for j, hit in enumerate(hits):
            live = jnp.concatenate(
                [jnp.broadcast_to(hit[r : r + 1], (BZ, LANES)) for r in range(slabs)], axis=0
            )
            span = pl.ds(j * LANES, LANES)
            total = jnp.zeros((depth_len, LANES), jnp.float32)
            for x in range(slices):
                cell = density_ref[x, :, span] * live
                bundle_ref[x, :, span] = cell
                total = total + cell
            column_ref[:, span] = total
            sums.append(total)
        moves[2].wait()
        lane = lane_iota((depth_len, LANES))
        low = [jnp.zeros((depth_len, LANES), jnp.float32) for _ in range(tiles)]
        high = [jnp.zeros((depth_len, LANES), jnp.float32) for _ in range(tiles)]
        for g in range(1 + colours):
            tile, shift = place(g)
            if g == 0:
                left, right = sums[0], sums[-1]
            else:
                owner = depth if g <= mine else 1 - depth
                c = owner * mine + (g - 1) % mine
                left = lamp_ref[c, :, pl.ds(0, LANES)]
                right = lamp_ref[c, :, pl.ds(height_len - LANES, LANES)]
            if shift:
                left = pltpu.roll(left, shift, 1)
                right = pltpu.roll(right, LANES - shift, 1)
            low[tile] = jnp.where((lane >= shift) & (lane < shift + halo), left, low[tile])
            high[tile] = jnp.where(
                (lane >= LANES - shift - halo) & (lane < LANES - shift), right, high[tile]
            )
        even_place = height % 2 == 0
        for t in range(tiles):
            span = pl.ds(t * LANES, LANES)
            even_ref[:, span] = jnp.where(even_place, high[t], low[t])
            odd_ref[:, span] = jnp.where(even_place, low[t], high[t])
        for move in moves[3:]:
            move.wait()

    bundle, column, edge_even, edge_odd, dirs, exts, blurs, albedos = pl.pallas_call(
        sums_kernel,
        name="sums",
        compiler_params=GRANT,
        in_specs=[HBM] * 7,
        out_specs=[VMEM] * 4 + [SMEM] * 4,
        out_shape=(
            pltpu.VMEM((slices + mine, depth_len, height_len), jnp.float32),
            pltpu.VMEM((depth_len, height_len), jnp.float32),
            pltpu.VMEM((depth_len, tiles * LANES), jnp.float32),
            pltpu.VMEM((depth_len, tiles * LANES), jnp.float32),
            pltpu.SMEM(light_dir.shape, jnp.int32),
            pltpu.SMEM(extinction.shape, jnp.float32),
            pltpu.SMEM(blur_weights.shape, jnp.float32),
            pltpu.SMEM(albedo.shape, jnp.float32),
        ),
        scratch_shapes=[
            pltpu.VMEM(density.shape, jnp.float32),
            pltpu.VMEM(active_list.shape, jnp.int32),
            pltpu.VMEM(lamp_plane.shape, jnp.float32),
            pltpu.SemaphoreType.DMA((8,)),
        ],
    )(*in_hbm(density, active_list, lamp_plane, light_dir, extinction, blur_weights, albedo))

    swap = [(0, 1), (1, 0)]
    theirs = lax.ppermute(bundle, "depth", swap)
    got_even = lax.ppermute(edge_even, "height", swaps(0, columns))
    got_odd = lax.ppermute(edge_odd, "height", swaps(1, columns))

    def gains_body(dir_ref, ext_ref, cells_ref, gain_ref, through_ref, cells, earlier):
        depth = lax.axis_index("depth")
        for j in range(blocks):
            running = jnp.zeros((depth_len, LANES), jnp.float32)
            for x in range(slices):
                rows = pl.ds(x * depth_len, depth_len)
                cell = cells_ref[x, :, pl.ds(j * LANES, LANES)]
                cells[j, rows, :] = cell
                earlier[j, rows, :] = running
                running = running + cell
            earlier[j, pl.ds(slices * depth_len, depth_len), :] = running
        down = [dir_ref[depth * mine + i] == 1 for i in range(mine)]
        rate = [-ext_ref[depth * mine + i] for i in range(mine)]

        def one_depth(z, through):
            passed = []
            for j in range(blocks):
                span = pl.ds(j * LANES, LANES)
                cell = cells[j, pl.ds(z, slices, stride=depth_len), :]
                before_up = earlier[j, pl.ds(z, slices, stride=depth_len), :]
                total = earlier[j, pl.ds(slices * depth_len + z, 1), :]
                before_down = total - before_up - cell
                kept = jnp.exp(cell * (-6.0 / full))
                weight = through[j] * (1.0 - kept)
                for i in range(mine):
                    before = jnp.where(down[i], before_down, before_up)
                    gain_ref[i, z, :, span] = weight * jnp.exp(rate[i] * before)
                passed.append(through[j] * kept)
            return tuple(passed)

        start = tuple(jnp.ones((slices, LANES), jnp.float32) for _ in range(blocks))
        for j, value in enumerate(lax.fori_loop(0, depth_len, one_depth, start)):
            through_ref[:, pl.ds(j * LANES, LANES)] = value

    gains_shape = (
        pltpu.VMEM((mine, depth_len, slices, height_len), jnp.float32),
        pltpu.VMEM((slices, height_len), jnp.float32),
    )
    gains_scratch = [
        pltpu.VMEM((blocks, slices * depth_len, LANES), jnp.float32),
        pltpu.VMEM((blocks, (slices + 1) * depth_len, LANES), jnp.float32),
    ]

    def near_kernel(dir_ref, ext_ref, blur_ref, cells_ref, gain_ref, through_ref, taps_ref, *scratch):
        depth = lax.axis_index("depth")
        shape = (full, LANES)
        lane = lane_iota(shape)
        offset = lane % full - lax.broadcasted_iota(jnp.int32, shape, 0) + TAPS // 2
        for i in range(mine):
            c = depth * mine + i
            norm = blur_ref[c, 0]
            for tap in range(1, TAPS * TAPS):
                norm = norm + blur_ref[c, tap]
            inverse = 1.0 / jnp.full(shape, norm, jnp.float32)
            for b in range(TAPS):
                band = jnp.zeros(shape, jnp.float32)
                for a in range(TAPS):
                    band = jnp.where(offset == a, blur_ref[c, a * TAPS + b], band)
                band = band * inverse
                high = band.astype(jnp.bfloat16).astype(jnp.float32)
                band = jnp.where(lane < 2 * full, high, band - high)
                taps_ref[i, pl.ds(b * full, full), :] = band.astype(jnp.bfloat16)[:, : 3 * full]
        gains_body(dir_ref, ext_ref, cells_ref, gain_ref, through_ref, *scratch)

    gain_near, through_near, taps = pl.pallas_call(
        near_kernel,
        name="near_gains",
        compiler_params=GRANT,
        in_specs=[SMEM] * 3 + [VMEM],
        out_shape=gains_shape + (pltpu.VMEM((mine, TAPS * full, 3 * full), jnp.bfloat16),),
        scratch_shapes=gains_scratch,
    )(*in_smem(dirs, exts, blurs), *in_vmem(bundle))

    def widen_kernel(column_ref, even_ref, odd_ref, wide_ref, halos_ref):
        even_place = lax.axis_index("height") % 2 == 0
        lane = lane_iota((depth_len, LANES))
        for t in range(tiles):
            span = pl.ds(t * LANES, LANES)
            a, b = even_ref[:, span], odd_ref[:, span]
            from_right = jnp.where(even_place, a, b)
            from_left = jnp.where(even_place, b, a)
            halos_ref[:, span] = from_right
            halos_ref[:, pl.ds((tiles + t) * LANES, LANES)] = from_left
            if t == 0:
                edge = jnp.where(
                    lane < halo, from_right, jnp.where(lane >= LANES - halo, from_left, 0.0)
                )
                wide_ref[:, pl.ds(height_len, LANES)] = edge
        wide_ref[:, pl.ds(0, height_len)] = column_ref[...]

    wide_column, halos = pl.pallas_call(
        widen_kernel,
        name="widen",
        compiler_params=GRANT,
        out_shape=(
            pltpu.VMEM((depth_len, wide), jnp.float32),
            pltpu.VMEM((depth_len, 2 * tiles * LANES), jnp.float32),
        ),
    )(*in_vmem(column, got_even, got_odd))

    near = []
    for k in range(1, chain):
        near.append(lax.ppermute(wide_column, "light", light_pairs(k, chain)))

    gain_far, through_far = pl.pallas_call(
        gains_body,
        name="far_gains",
        compiler_params=GRANT,
        in_specs=[SMEM] * 2 + [VMEM],
        out_shape=gains_shape,
        scratch_shapes=gains_scratch,
    )(*in_smem(dirs, exts), *in_vmem(theirs))

    def join_kernel(*refs):
        out_ref = refs[-1]
        for k, ref in enumerate(refs[: chain - 1]):
            out_ref[pl.ds(k * depth_len, depth_len), :] = ref[...]
        for t in range(2 * tiles):
            row, lane = divmod(t * LANES, wide)
            out_ref[pl.ds((chain - 1 + row) * depth_len, depth_len), pl.ds(lane, LANES)] = refs[
                chain - 1
            ][:, pl.ds(t * LANES, LANES)]

    parcel = pl.pallas_call(
        join_kernel,
        name="join",
        compiler_params=GRANT,
        out_shape=pltpu.VMEM(((chain - 1) * depth_len + halo_rows, wide), jnp.float32),
    )(*in_vmem(*near, halos))
    far = lax.ppermute(parcel, "depth", swap)

    def chain_kernel(
        dir_ref, ext_ref, albedo_ref, lamp_ref, theirs_ref, near_ref, far_ref, taps_ref,
        gain_near_ref, through_near_ref, gain_far_ref, through_far_ref, out_ref, walls, plane, lit,
    ):
        light = lax.axis_index("light")
        depth = lax.axis_index("depth")
        height = lax.axis_index("height")
        own_row = pl.multiple_of(depth * depth_len, BZ)
        other_row = pl.multiple_of((1 - depth) * depth_len, BZ)
        for k in range(1, chain):
            source = peer(light, k, chain)
            rows = pl.ds((k - 1) * depth_len, depth_len)
            walls[source, pl.ds(own_row, depth_len), :] = near_ref[rows, :]
            walls[source, pl.ds(other_row, depth_len), :] = far_ref[rows, :]
        lane = lane_iota((depth_len, LANES))

        def halo_tile(ref, t):
            row, first = divmod(t * LANES, wide)
            return ref[pl.ds((chain - 1 + row) * depth_len, depth_len), pl.ds(first, LANES)]

        for i in range(mine):
            for row, group, edges, body in (
                (own_row, 1 + i, near_ref, lamp_ref[depth * mine + i]),
                (other_row, 1 + mine + i, far_ref, theirs_ref[slices + i]),
            ):
                tile, shift = place(group)
                from_right = halo_tile(edges, tile)
                from_left = halo_tile(edges, tiles + tile)
                if shift:
                    from_right = pltpu.roll(from_right, LANES - shift, 1)
                    from_left = pltpu.roll(from_left, shift, 1)
                edge = jnp.where(
                    lane < halo, from_right, jnp.where(lane >= LANES - halo, from_left, 0.0)
                )
                plane[i, pl.ds(row, depth_len), pl.ds(0, height_len)] = body
                plane[i, pl.ds(row, depth_len), pl.ds(height_len, LANES)] = edge
        wide_lane = lane_iota((1, wide))
        inside = (
            (wide_lane < height_len)
            | ((wide_lane < height_len + LANES // 2) & (height < columns - 1))
            | ((wide_lane >= height_len + LANES // 2) & (height > 0))
        )
        inside = jnp.where(inside, 1.0, 0.0)
        down = [dir_ref[depth * mine + i] == 1 for i in range(mine)]
        steps = [jnp.where(d, chain - 1 - light, light) for d in down]
        rate = [-ext_ref[depth * mine + i] for i in range(mine)]

        def one_step(s, carry):
            for i in range(mine):
                wall = walls[jnp.where(down[i], chain - 1 - s, s)]
                before = plane[i]
                high, low = split(before * (jnp.exp(rate[i] * wall) * inside))
                bands = jnp.dot(
                    taps_ref[i],
                    jnp.concatenate([high, low, high], axis=0),
                    preferred_element_type=jnp.float32,
                )
                after = None
                for b in range(TAPS):
                    part = bands[b * full : (b + 1) * full]
                    if b != TAPS // 2:
                        part = pltpu.roll(part, (TAPS // 2 - b) % wide, 1)
                    after = part if after is None else after + part
                plane[i] = jnp.where(s < steps[i], after, before)
            return carry

        lax.fori_loop(0, jnp.maximum(light, chain - 1 - light), one_step, 0)
        in_front = depth == 0
        for i in range(mine):
            for half, row in enumerate((own_row, other_row)):
                lit[half, i] = plane[i, pl.ds(row, depth_len), pl.ds(0, height_len)]
            shade = albedo_ref[depth * mine + i]
            for j in range(blocks):
                span = pl.ds(j * LANES, LANES)
                sums = []
                for half, gain in enumerate((gain_near_ref, gain_far_ref)):
                    parts = [jnp.zeros((slices, LANES), jnp.float32) for _ in range(2)]
                    for z in range(depth_len):
                        light_row = lit[half, i, pl.ds(z, 1), span]
                        parts[z % 2] = parts[z % 2] + light_row * gain[i, z, :, span]
                    sums.append(parts[0] + parts[1])
                front = jnp.where(in_front, sums[0], sums[1])
                back = jnp.where(in_front, sums[1], sums[0])
                through = jnp.where(in_front, through_near_ref[:, span], through_far_ref[:, span])
                out_ref[i, :, span] = shade * (front + through * back)

    return pl.pallas_call(
        chain_kernel,
        name="chain",
        compiler_params=GRANT,
        in_specs=[SMEM] * 3 + [VMEM] * 9,
        out_specs=VMEM,
        out_shape=jax.ShapeDtypeStruct((mine, slices, height_len), jnp.float32),
        scratch_shapes=[
            pltpu.VMEM((chain, full, wide), jnp.float32),
            pltpu.VMEM((mine, full, wide), jnp.float32),
            pltpu.VMEM((groups, mine, depth_len, height_len), jnp.float32),
        ],
    )(
        *in_smem(dirs, exts, albedos),
        *in_vmem(lamp_plane, theirs, parcel, far, taps),
        *in_vmem(gain_near, through_near, gain_far, through_far),
    )


def solution(mesh):
    in_specs = (
        P("light", "depth", "height"),
        P("depth", None),
        P(),
        P(None, "depth", "height"),
        P(),
        P(),
        P(),
    )
    out_specs = P("depth", "light", "height")

    return jax.shard_map(local, mesh=mesh, in_specs=in_specs, out_specs=out_specs, check_vma=False)
```

```python
import jax
import jax.numpy as jnp
from jax import lax
from jax.experimental import pallas as pl
from jax.experimental.pallas import tpu as pltpu
from jax.sharding import PartitionSpec as P

BZ = 8
LANES = 128
TAPS = 5
GRANT = pltpu.CompilerParams(vmem_limit_bytes=24 << 20)
SMEM = pl.BlockSpec(memory_space=pltpu.SMEM)
VMEM = pl.BlockSpec(memory_space=pltpu.VMEM)
HBM = pl.BlockSpec(memory_space=pltpu.HBM)


def pairs_even(count):
    return [(i, i ^ 1) for i in range(count) if (i ^ 1) < count]


def pairs_odd(count):
    inner = [(i, i + 1) for i in range(1, count - 1, 2)]
    return inner + [(b, a) for a, b in inner]


def peer(position, k, count):
    if count & (count - 1) == 0:
        return position ^ k
    return (position - k) % count


def light_pairs(k, count):
    return [(peer(i, k, count), i) for i in range(count)]


def lane_iota(shape):
    return lax.broadcasted_iota(jnp.int32, shape, len(shape) - 1)


def in_vmem(*values):
    return [pltpu.with_memory_space_constraint(v, pltpu.VMEM) for v in values]


def in_hbm(*values):
    return [pltpu.with_memory_space_constraint(v, pltpu.HBM) for v in values]


def in_smem(*values):
    return [pltpu.with_memory_space_constraint(v, pltpu.SMEM) for v in values]


def split(value):
    high = value.astype(jnp.bfloat16)
    return high, (value - high.astype(jnp.float32)).astype(jnp.bfloat16)


def local(density, active_list, light_dir, lamp_plane, extinction, blur_weights, albedo):
    colours = extinction.shape[0]
    slices, depth_len, height_len = density.shape
    chain = lax.axis_size("light")
    groups = lax.axis_size("depth")
    columns = lax.axis_size("height")
    assert groups == 2
    mine = colours // groups
    full = depth_len * groups
    halo = 2 * (chain - 1)
    assert 2 * halo <= LANES
    wide = height_len + LANES
    per_tile = LANES // halo
    tiles = -(-(1 + colours) // per_tile)
    assert 2 * tiles * LANES <= wide * chain
    blocks = height_len // LANES
    slabs = depth_len // BZ
    halo_rows = -(-2 * tiles * LANES // wide) * depth_len

    def place(g):
        return g // per_tile, (g % per_tile) * halo

    def sums_kernel(
        density_hbm, active_hbm, lamp_hbm, dir_hbm, ext_hbm, blur_hbm, albedo_hbm,
        bundle_ref, column_ref, even_ref, odd_ref, dir_ref, ext_ref, blur_ref, albedo_ref,
        density_ref, active_ref, lamp_ref, arrivals,
    ):
        light = lax.axis_index("light")
        depth = lax.axis_index("depth")
        height = lax.axis_index("height")
        size = slices
        chunks = [pl.ds(x, min(size, slices - x)) for x in range(0, slices, size)]
        moves = [
            pltpu.make_async_copy(source, target, arrivals.at[i])
            for i, (source, target) in enumerate(
                (
                    (active_hbm, active_ref),
                    *((density_hbm.at[part], density_ref.at[part]) for part in chunks),
                    (lamp_hbm, lamp_ref),
                    (lamp_hbm.at[pl.ds((1 - depth) * mine, mine)], bundle_ref.at[pl.ds(slices, mine)]),
                    (dir_hbm, dir_ref),
                    (ext_hbm, ext_ref),
                    (blur_hbm, blur_ref),
                    (albedo_hbm, albedo_ref),
                )
            )
        ]
        for move in moves:
            move.start()
        moves[0].wait()
        listed = active_ref[...]
        first_brick = (light * columns + height) * blocks
        lives = []
        for j in range(blocks):
            hit = jnp.max(
                jnp.where(listed == first_brick + j, 1.0, 0.0), axis=1, keepdims=True
            )
            lives.append(
                jnp.concatenate(
                    [jnp.broadcast_to(hit[r : r + 1], (BZ, LANES)) for r in range(slabs)], axis=0
                )
            )
        sums = [None] * blocks
        for part, move in zip(chunks, moves[1:]):
            move.wait()
            for x in range(part.start, part.start + part.size):
                for j in range(blocks):
                    span = pl.ds(j * LANES, LANES)
                    cell = density_ref[x, :, span] * lives[j]
                    bundle_ref[x, :, span] = cell
                    sums[j] = cell if x == 0 else sums[j] + cell
        for j in range(blocks):
            column_ref[:, pl.ds(j * LANES, LANES)] = sums[j]
        moves[1 + len(chunks)].wait()
        lane = lane_iota((depth_len, LANES))
        low = [jnp.zeros((depth_len, LANES), jnp.float32) for _ in range(tiles)]
        high = [jnp.zeros((depth_len, LANES), jnp.float32) for _ in range(tiles)]
        for g in range(1 + colours):
            tile, shift = place(g)
            if g == 0:
                left, right = sums[0], sums[-1]
            else:
                owner = depth if g <= mine else 1 - depth
                c = owner * mine + (g - 1) % mine
                left = lamp_ref[c, :, pl.ds(0, LANES)]
                right = lamp_ref[c, :, pl.ds(height_len - LANES, LANES)]
            if shift:
                left = pltpu.roll(left, shift, 1)
                right = pltpu.roll(right, LANES - shift, 1)
            low[tile] = jnp.where((lane >= shift) & (lane < shift + halo), left, low[tile])
            high[tile] = jnp.where(
                (lane >= LANES - shift - halo) & (lane < LANES - shift), right, high[tile]
            )
        even_place = height % 2 == 0
        for t in range(tiles):
            span = pl.ds(t * LANES, LANES)
            even_ref[:, span] = jnp.where(even_place, high[t], low[t])
            odd_ref[:, span] = jnp.where(even_place, low[t], high[t])
        for move in moves[2 + len(chunks) :]:
            move.wait()

    bundle, column, edge_even, edge_odd, dirs, exts, blurs, albedos = pl.pallas_call(
        sums_kernel,
        name="sums",
        compiler_params=GRANT,
        in_specs=[HBM] * 7,
        out_specs=[VMEM] * 4 + [SMEM] * 4,
        out_shape=(
            pltpu.VMEM((slices + mine, depth_len, height_len), jnp.float32),
            pltpu.VMEM((depth_len, height_len), jnp.float32),
            pltpu.VMEM((depth_len, tiles * LANES), jnp.float32),
            pltpu.VMEM((depth_len, tiles * LANES), jnp.float32),
            pltpu.SMEM(light_dir.shape, jnp.int32),
            pltpu.SMEM(extinction.shape, jnp.float32),
            pltpu.SMEM(blur_weights.shape, jnp.float32),
            pltpu.SMEM(albedo.shape, jnp.float32),
        ),
        scratch_shapes=[
            pltpu.VMEM(density.shape, jnp.float32),
            pltpu.VMEM(active_list.shape, jnp.int32),
            pltpu.VMEM(lamp_plane.shape, jnp.float32),
            pltpu.SemaphoreType.DMA((8,)),
        ],
    )(*in_hbm(density, active_list, lamp_plane, light_dir, extinction, blur_weights, albedo))

    swap = [(0, 1), (1, 0)]
    theirs = lax.ppermute(bundle, "depth", swap)
    got_even = lax.ppermute(edge_even, "height", pairs_even(columns))
    got_odd = lax.ppermute(edge_odd, "height", pairs_odd(columns))

    def gains_body(dir_ref, ext_ref, cells_ref, gain_ref, through_ref, cells, earlier):
        depth = lax.axis_index("depth")
        for j in range(blocks):
            running = jnp.zeros((depth_len, LANES), jnp.float32)
            for x in range(slices):
                rows = pl.ds(x * depth_len, depth_len)
                cell = cells_ref[x, :, pl.ds(j * LANES, LANES)]
                cells[j, rows, :] = cell
                earlier[j, rows, :] = running
                running = running + cell
            earlier[j, pl.ds(slices * depth_len, depth_len), :] = running
        down = [dir_ref[depth * mine + i] == 1 for i in range(mine)]
        rate = [-ext_ref[depth * mine + i] for i in range(mine)]

        def one_depth(z, through):
            passed = []
            for j in range(blocks):
                span = pl.ds(j * LANES, LANES)
                cell = cells[j, pl.ds(z, slices, stride=depth_len), :]
                before_up = earlier[j, pl.ds(z, slices, stride=depth_len), :]
                total = earlier[j, pl.ds(slices * depth_len + z, 1), :]
                before_down = total - before_up - cell
                kept = jnp.exp(cell * (-6.0 / full))
                weight = through[j] * (1.0 - kept)
                for i in range(mine):
                    before = jnp.where(down[i], before_down, before_up)
                    gain_ref[i, z, :, span] = weight * jnp.exp(rate[i] * before)
                passed.append(through[j] * kept)
            return tuple(passed)

        start = tuple(jnp.ones((slices, LANES), jnp.float32) for _ in range(blocks))
        for j, value in enumerate(lax.fori_loop(0, depth_len, one_depth, start)):
            through_ref[:, pl.ds(j * LANES, LANES)] = value

    gains_shape = (
        pltpu.VMEM((mine, depth_len, slices, height_len), jnp.float32),
        pltpu.VMEM((slices, height_len), jnp.float32),
    )
    gains_scratch = [
        pltpu.VMEM((blocks, slices * depth_len, LANES), jnp.float32),
        pltpu.VMEM((blocks, (slices + 1) * depth_len, LANES), jnp.float32),
    ]

    def near_kernel(dir_ref, ext_ref, blur_ref, cells_ref, gain_ref, through_ref, taps_ref, *scratch):
        depth = lax.axis_index("depth")
        shape = (full, LANES)
        lane = lane_iota(shape)
        offset = lane % full - lax.broadcasted_iota(jnp.int32, shape, 0) + TAPS // 2
        for i in range(mine):
            c = depth * mine + i
            norm = blur_ref[c, 0]
            for tap in range(1, TAPS * TAPS):
                norm = norm + blur_ref[c, tap]
            inverse = 1.0 / jnp.full(shape, norm, jnp.float32)
            for b in range(TAPS):
                band = jnp.zeros(shape, jnp.float32)
                for a in range(TAPS):
                    band = jnp.where(offset == a, blur_ref[c, a * TAPS + b], band)
                band = band * inverse
                high = band.astype(jnp.bfloat16).astype(jnp.float32)
                band = jnp.where(lane < 2 * full, high, band - high)
                taps_ref[i, pl.ds(b * full, full), :] = band.astype(jnp.bfloat16)[:, : 3 * full]
        gains_body(dir_ref, ext_ref, cells_ref, gain_ref, through_ref, *scratch)

    gain_near, through_near, taps = pl.pallas_call(
        near_kernel,
        name="near_gains",
        compiler_params=GRANT,
        in_specs=[SMEM] * 3 + [VMEM],
        out_shape=gains_shape + (pltpu.VMEM((mine, TAPS * full, 3 * full), jnp.bfloat16),),
        scratch_shapes=gains_scratch,
    )(*in_smem(dirs, exts, blurs), *in_vmem(bundle))

    def widen_kernel(column_ref, even_ref, odd_ref, wide_ref, halos_ref):
        even_place = lax.axis_index("height") % 2 == 0
        lane = lane_iota((depth_len, LANES))
        for t in range(tiles):
            span = pl.ds(t * LANES, LANES)
            a, b = even_ref[:, span], odd_ref[:, span]
            from_right = jnp.where(even_place, a, b)
            from_left = jnp.where(even_place, b, a)
            halos_ref[:, span] = from_right
            halos_ref[:, pl.ds((tiles + t) * LANES, LANES)] = from_left
            if t == 0:
                edge = jnp.where(
                    lane < halo, from_right, jnp.where(lane >= LANES - halo, from_left, 0.0)
                )
                wide_ref[:, pl.ds(height_len, LANES)] = edge
        wide_ref[:, pl.ds(0, height_len)] = column_ref[...]

    wide_column, halos = pl.pallas_call(
        widen_kernel,
        name="widen",
        compiler_params=GRANT,
        out_shape=(
            pltpu.VMEM((depth_len, wide), jnp.float32),
            pltpu.VMEM((depth_len, 2 * tiles * LANES), jnp.float32),
        ),
    )(*in_vmem(column, got_even, got_odd))

    near = []
    for k in range(1, chain):
        near.append(lax.ppermute(wide_column, "light", light_pairs(k, chain)))

    gain_far, through_far = pl.pallas_call(
        gains_body,
        name="far_gains",
        compiler_params=GRANT,
        in_specs=[SMEM] * 2 + [VMEM],
        out_shape=gains_shape,
        scratch_shapes=gains_scratch,
    )(*in_smem(dirs, exts), *in_vmem(theirs))

    joined = (chain - 2) * depth_len

    def join_kernel(*refs):
        out_ref = refs[-1]
        for k, ref in enumerate(refs[: chain - 2]):
            out_ref[pl.ds(k * depth_len, depth_len), :] = ref[...]
        for t in range(2 * tiles):
            row, lane = divmod(t * LANES, wide)
            out_ref[pl.ds(joined + row * depth_len, depth_len), pl.ds(lane, LANES)] = refs[
                chain - 2
            ][:, pl.ds(t * LANES, LANES)]

    parcel = pl.pallas_call(
        join_kernel,
        name="join",
        compiler_params=GRANT,
        out_shape=pltpu.VMEM((joined + halo_rows, wide), jnp.float32),
    )(*in_vmem(*near[1:], halos))
    far_parcel = lax.ppermute(parcel, "depth", swap)
    far_last = lax.ppermute(near[0], "depth", swap)

    def chain_kernel(
        dir_ref, ext_ref, albedo_ref, lamp_ref, theirs_ref, near_last_ref, far_last_ref,
        near_ref, far_ref, taps_ref,
        gain_near_ref, through_near_ref, gain_far_ref, through_far_ref, out_ref, walls, plane, lit,
    ):
        light = lax.axis_index("light")
        depth = lax.axis_index("depth")
        height = lax.axis_index("height")
        own_row = pl.multiple_of(depth * depth_len, BZ)
        other_row = pl.multiple_of((1 - depth) * depth_len, BZ)
        for k in range(1, chain):
            source = peer(light, k, chain)
            for row, last, others in (
                (own_row, near_last_ref, near_ref),
                (other_row, far_last_ref, far_ref),
            ):
                if k > 1:
                    column = others[pl.ds((k - 2) * depth_len, depth_len), :]
                else:
                    column = last[...]
                walls[source, pl.ds(row, depth_len), :] = column
        lane = lane_iota((depth_len, LANES))

        def halo_tile(ref, t):
            row, first = divmod(t * LANES, wide)
            return ref[pl.ds(joined + row * depth_len, depth_len), pl.ds(first, LANES)]

        down = [dir_ref[depth * mine + i] for i in range(mine)]
        ups = mine - sum(down[1:], down[0])
        rank, ups_seen, downs_seen = [], 0, 0
        for i in range(mine):
            rank.append(jnp.where(down[i] == 1, ups + downs_seen, ups_seen))
            ups_seen = ups_seen + 1 - down[i]
            downs_seen = downs_seen + down[i]
        order = [
            sum((jnp.where(rank[i] == r, i, 0) for i in range(1, mine)), jnp.int32(0))
            for r in range(mine)
        ]
        for i in range(mine):
            for row, group, edges, body in (
                (own_row, 1 + i, near_ref, lamp_ref[depth * mine + i]),
                (other_row, 1 + mine + i, far_ref, theirs_ref[slices + i]),
            ):
                tile, shift = place(group)
                from_right = halo_tile(edges, tile)
                from_left = halo_tile(edges, tiles + tile)
                if shift:
                    from_right = pltpu.roll(from_right, LANES - shift, 1)
                    from_left = pltpu.roll(from_left, shift, 1)
                edge = jnp.where(
                    lane < halo, from_right, jnp.where(lane >= LANES - halo, from_left, 0.0)
                )
                plane[rank[i], pl.ds(row, depth_len), pl.ds(0, height_len)] = body
                plane[rank[i], pl.ds(row, depth_len), pl.ds(height_len, LANES)] = edge
        wide_lane = lane_iota((1, wide))
        inside = (
            (wide_lane < height_len)
            | ((wide_lane < height_len + LANES // 2) & (height < columns - 1))
            | ((wide_lane >= height_len + LANES // 2) & (height > 0))
        )
        inside = jnp.where(inside, 1.0, 0.0)
        ups_steps, down_steps = light, chain - 1 - light
        shared = jnp.minimum(ups_steps, down_steps)
        longest = jnp.maximum(ups_steps, down_steps)
        ups_longer = ups_steps > down_steps
        alone = jnp.where(ups_longer, ups, mine - ups)
        first_alone = jnp.where(ups_longer, 0, ups)
        as_pair = alone <= 2

        def advance(places, s):
            results = []
            for place_in in places:
                c = depth * mine + order[place_in] if isinstance(place_in, int) else None
                if c is None:
                    c = depth * mine + chosen(place_in)
                goes_down = place_in >= ups
                wall = walls[jnp.where(goes_down, chain - 1 - s, s)]
                before = plane[place_in]
                high, low = split(before * (jnp.exp(-ext_ref[c] * wall) * inside))
                bands = jnp.dot(
                    taps_ref[c - depth * mine],
                    jnp.concatenate([high, low, high], axis=0),
                    preferred_element_type=jnp.float32,
                )
                after = None
                for b in range(TAPS):
                    part = bands[b * full : (b + 1) * full]
                    if b != TAPS // 2:
                        part = pltpu.roll(part, (TAPS // 2 - b) % wide, 1)
                    after = part if after is None else after + part
                active = s < jnp.where(goes_down, down_steps, ups_steps)
                results.append(jnp.where(active, after, before))
            for place_in, after in zip(places, results):
                plane[place_in] = after

        def chosen(place_in):
            c = order[0]
            for i in range(1, mine):
                c = jnp.where(place_in == i, order[i], c)
            return c

        def all_step(s, carry):
            advance(range(mine), s)
            return carry

        def pair_step(s, carry):
            advance((first_alone, first_alone + jnp.maximum(alone - 1, 0)), s)
            return carry

        lax.fori_loop(0, jnp.where(as_pair, shared, longest), all_step, 0)
        lax.fori_loop(
            shared, jnp.where(as_pair & (alone > 0), longest, shared), pair_step, 0
        )
        in_front = depth == 0
        for i in range(mine):
            for half, row in enumerate((own_row, other_row)):
                lit[half, i] = plane[rank[i], pl.ds(row, depth_len), pl.ds(0, height_len)]
            shade = albedo_ref[depth * mine + i]
            sums = []
            for half, gain in enumerate((gain_near_ref, gain_far_ref)):
                parts = [None] * blocks
                for z in range(depth_len):
                    for j in range(blocks):
                        span = pl.ds(j * LANES, LANES)
                        part = lit[half, i, pl.ds(z, 1), span] * gain[i, z, :, span]
                        parts[j] = part if z == 0 else parts[j] + part
                sums.append(parts)
            for j in range(blocks):
                span = pl.ds(j * LANES, LANES)
                front = jnp.where(in_front, sums[0][j], sums[1][j])
                back = jnp.where(in_front, sums[1][j], sums[0][j])
                through = jnp.where(in_front, through_near_ref[:, span], through_far_ref[:, span])
                out_ref[i, :, span] = shade * (front + through * back)

    return pl.pallas_call(
        chain_kernel,
        name="chain",
        compiler_params=GRANT,
        in_specs=[SMEM] * 3 + [VMEM] * 11,
        out_specs=VMEM,
        out_shape=jax.ShapeDtypeStruct((mine, slices, height_len), jnp.float32),
        scratch_shapes=[
            pltpu.VMEM((chain, full, wide), jnp.float32),
            pltpu.VMEM((mine, full, wide), jnp.float32),
            pltpu.VMEM((groups, mine, depth_len, height_len), jnp.float32),
        ],
    )(
        *in_smem(dirs, exts, albedos),
        *in_vmem(lamp_plane, theirs, near[0], far_last, parcel, far_parcel, taps),
        *in_vmem(gain_near, through_near, gain_far, through_far),
    )


def solution(mesh):
    in_specs = (
        P("light", "depth", "height"),
        P("depth", None),
        P(),
        P(None, "depth", "height"),
        P(),
        P(),
        P(),
    )
    out_specs = P("depth", "light", "height")

    return jax.shard_map(local, mesh=mesh, in_specs=in_specs, out_specs=out_specs, check_vma=False)
```

```python
import jax
import jax.numpy as jnp
from jax import lax
from jax.experimental import pallas as pl
from jax.experimental.pallas import tpu as pltpu
from jax.sharding import PartitionSpec as P

BZ = 8
LANES = 128
TAPS = 5
GRANT = pltpu.CompilerParams(vmem_limit_bytes=24 << 20)
SMEM = pl.BlockSpec(memory_space=pltpu.SMEM)
VMEM = pl.BlockSpec(memory_space=pltpu.VMEM)
HBM = pl.BlockSpec(memory_space=pltpu.HBM)


def ring(step, count):
    return [(i, (i + step) % count) for i in range(count)]


def peer(position, k, count):
    if count & (count - 1) == 0:
        return position ^ k
    return (position - k) % count


def light_pairs(k, count):
    return [(peer(i, k, count), i) for i in range(count)]


def lane_iota(shape):
    return lax.broadcasted_iota(jnp.int32, shape, len(shape) - 1)


def in_vmem(*values):
    return [pltpu.with_memory_space_constraint(v, pltpu.VMEM) for v in values]


def in_hbm(*values):
    return [pltpu.with_memory_space_constraint(v, pltpu.HBM) for v in values]


def in_smem(*values):
    return [pltpu.with_memory_space_constraint(v, pltpu.SMEM) for v in values]


def split(value):
    high = value.astype(jnp.bfloat16)
    return high, (value - high.astype(jnp.float32)).astype(jnp.bfloat16)


def local(density, active_list, light_dir, lamp_plane, extinction, blur_weights, albedo):
    colours = extinction.shape[0]
    slices, depth_len, height_len = density.shape
    chain = lax.axis_size("light")
    groups = lax.axis_size("depth")
    columns = lax.axis_size("height")
    assert groups == 2
    mine = colours // groups
    full = depth_len * groups
    halo = 2 * (chain - 1)
    assert 2 * halo <= LANES
    wide = height_len + LANES
    per_tile = LANES // halo
    tiles = -(-(1 + colours) // per_tile)
    assert 2 * tiles * LANES <= wide * chain
    blocks = height_len // LANES
    slabs = depth_len // BZ
    halo_rows = -(-2 * tiles * LANES // wide) * depth_len

    def place(g):
        return g // per_tile, (g % per_tile) * halo

    def sums_kernel(
        density_hbm, active_hbm, lamp_hbm, dir_hbm, ext_hbm, blur_hbm, albedo_hbm,
        bundle_ref, column_ref, high_ref, low_ref, dir_ref, ext_ref, blur_ref, albedo_ref,
        density_ref, active_ref, lamp_ref, arrivals,
    ):
        light = lax.axis_index("light")
        depth = lax.axis_index("depth")
        height = lax.axis_index("height")
        size = slices
        chunks = [pl.ds(x, min(size, slices - x)) for x in range(0, slices, size)]
        moves = [
            pltpu.make_async_copy(source, target, arrivals.at[i])
            for i, (source, target) in enumerate(
                (
                    (active_hbm, active_ref),
                    *((density_hbm.at[part], density_ref.at[part]) for part in chunks),
                    (lamp_hbm, lamp_ref),
                    (lamp_hbm.at[pl.ds((1 - depth) * mine, mine)], bundle_ref.at[pl.ds(slices, mine)]),
                    (dir_hbm, dir_ref),
                    (ext_hbm, ext_ref),
                    (blur_hbm, blur_ref),
                    (albedo_hbm, albedo_ref),
                )
            )
        ]
        for move in moves:
            move.start()
        moves[0].wait()
        listed = active_ref[...]
        first_brick = (light * columns + height) * blocks
        lives = []
        for j in range(blocks):
            hit = jnp.max(
                jnp.where(listed == first_brick + j, 1.0, 0.0), axis=1, keepdims=True
            )
            lives.append(
                jnp.concatenate(
                    [jnp.broadcast_to(hit[r : r + 1], (BZ, LANES)) for r in range(slabs)], axis=0
                )
            )
        sums = [None] * blocks
        for part, move in zip(chunks, moves[1:]):
            move.wait()
            for x in range(part.start, part.start + part.size):
                for j in range(blocks):
                    span = pl.ds(j * LANES, LANES)
                    cell = density_ref[x, :, span] * lives[j]
                    bundle_ref[x, :, span] = cell
                    sums[j] = cell if x == 0 else sums[j] + cell
        for j in range(blocks):
            column_ref[:, pl.ds(j * LANES, LANES)] = sums[j]
        moves[1 + len(chunks)].wait()
        lane = lane_iota((depth_len, LANES))
        low = [jnp.zeros((depth_len, LANES), jnp.float32) for _ in range(tiles)]
        high = [jnp.zeros((depth_len, LANES), jnp.float32) for _ in range(tiles)]
        for g in range(1 + colours):
            tile, shift = place(g)
            if g == 0:
                left, right = sums[0], sums[-1]
            else:
                owner = depth if g <= mine else 1 - depth
                c = owner * mine + (g - 1) % mine
                left = lamp_ref[c, :, pl.ds(0, LANES)]
                right = lamp_ref[c, :, pl.ds(height_len - LANES, LANES)]
            if shift:
                left = pltpu.roll(left, shift, 1)
                right = pltpu.roll(right, LANES - shift, 1)
            low[tile] = jnp.where((lane >= shift) & (lane < shift + halo), left, low[tile])
            high[tile] = jnp.where(
                (lane >= LANES - shift - halo) & (lane < LANES - shift), right, high[tile]
            )
        for t in range(tiles):
            span = pl.ds(t * LANES, LANES)
            high_ref[:, span] = high[t]
            low_ref[:, span] = low[t]
        for move in moves[2 + len(chunks) :]:
            move.wait()

    bundle, column, edge_high, edge_low, dirs, exts, blurs, albedos = pl.pallas_call(
        sums_kernel,
        name="sums",
        compiler_params=GRANT,
        in_specs=[HBM] * 7,
        out_specs=[VMEM] * 4 + [SMEM] * 4,
        out_shape=(
            pltpu.VMEM((slices + mine, depth_len, height_len), jnp.float32),
            pltpu.VMEM((depth_len, height_len), jnp.float32),
            pltpu.VMEM((depth_len, tiles * LANES), jnp.float32),
            pltpu.VMEM((depth_len, tiles * LANES), jnp.float32),
            pltpu.SMEM(light_dir.shape, jnp.int32),
            pltpu.SMEM(extinction.shape, jnp.float32),
            pltpu.SMEM(blur_weights.shape, jnp.float32),
            pltpu.SMEM(albedo.shape, jnp.float32),
        ),
        scratch_shapes=[
            pltpu.VMEM(density.shape, jnp.float32),
            pltpu.VMEM(active_list.shape, jnp.int32),
            pltpu.VMEM(lamp_plane.shape, jnp.float32),
            pltpu.SemaphoreType.DMA((8,)),
        ],
    )(*in_hbm(density, active_list, lamp_plane, light_dir, extinction, blur_weights, albedo))

    swap = [(0, 1), (1, 0)]
    theirs = lax.ppermute(bundle, "depth", swap)
    from_left = lax.ppermute(edge_high, "height", ring(1, columns))
    from_right = lax.ppermute(edge_low, "height", ring(-1, columns))

    def gains_body(dir_ref, ext_ref, cells_ref, gain_ref, through_ref, cells, earlier):
        depth = lax.axis_index("depth")
        for j in range(blocks):
            running = jnp.zeros((depth_len, LANES), jnp.float32)
            for x in range(slices):
                rows = pl.ds(x * depth_len, depth_len)
                cell = cells_ref[x, :, pl.ds(j * LANES, LANES)]
                cells[j, rows, :] = cell
                earlier[j, rows, :] = running
                running = running + cell
            earlier[j, pl.ds(slices * depth_len, depth_len), :] = running
        down = [dir_ref[depth * mine + i] == 1 for i in range(mine)]
        rate = [-ext_ref[depth * mine + i] for i in range(mine)]

        def one_depth(z, through):
            passed = []
            for j in range(blocks):
                span = pl.ds(j * LANES, LANES)
                cell = cells[j, pl.ds(z, slices, stride=depth_len), :]
                before_up = earlier[j, pl.ds(z, slices, stride=depth_len), :]
                total = earlier[j, pl.ds(slices * depth_len + z, 1), :]
                before_down = total - before_up - cell
                kept = jnp.exp(cell * (-6.0 / full))
                weight = through[j] * (1.0 - kept)
                for i in range(mine):
                    before = jnp.where(down[i], before_down, before_up)
                    gain_ref[i, z, :, span] = weight * jnp.exp(rate[i] * before)
                passed.append(through[j] * kept)
            return tuple(passed)

        start = tuple(jnp.ones((slices, LANES), jnp.float32) for _ in range(blocks))
        for j, value in enumerate(lax.fori_loop(0, depth_len, one_depth, start)):
            through_ref[:, pl.ds(j * LANES, LANES)] = value

    gains_shape = (
        pltpu.VMEM((mine, depth_len, slices, height_len), jnp.float32),
        pltpu.VMEM((slices, height_len), jnp.float32),
    )
    gains_scratch = [
        pltpu.VMEM((blocks, slices * depth_len, LANES), jnp.float32),
        pltpu.VMEM((blocks, (slices + 1) * depth_len, LANES), jnp.float32),
    ]

    def near_kernel(dir_ref, ext_ref, blur_ref, cells_ref, gain_ref, through_ref, taps_ref, *scratch):
        depth = lax.axis_index("depth")
        shape = (full, LANES)
        lane = lane_iota(shape)
        offset = lane % full - lax.broadcasted_iota(jnp.int32, shape, 0) + TAPS // 2
        for i in range(mine):
            c = depth * mine + i
            norm = blur_ref[c, 0]
            for tap in range(1, TAPS * TAPS):
                norm = norm + blur_ref[c, tap]
            inverse = 1.0 / jnp.full(shape, norm, jnp.float32)
            for b in range(TAPS):
                band = jnp.zeros(shape, jnp.float32)
                for a in range(TAPS):
                    band = jnp.where(offset == a, blur_ref[c, a * TAPS + b], band)
                band = band * inverse
                high = band.astype(jnp.bfloat16).astype(jnp.float32)
                band = jnp.where(lane < 2 * full, high, band - high)
                taps_ref[i, pl.ds(b * full, full), :] = band.astype(jnp.bfloat16)[:, : 3 * full]
        gains_body(dir_ref, ext_ref, cells_ref, gain_ref, through_ref, *scratch)

    gain_near, through_near, taps = pl.pallas_call(
        near_kernel,
        name="near_gains",
        compiler_params=GRANT,
        in_specs=[SMEM] * 3 + [VMEM],
        out_shape=gains_shape + (pltpu.VMEM((mine, TAPS * full, 3 * full), jnp.bfloat16),),
        scratch_shapes=gains_scratch,
    )(*in_smem(dirs, exts, blurs), *in_vmem(bundle))

    def widen_kernel(column_ref, left_ref, right_ref, wide_ref, halos_ref):
        lane = lane_iota((depth_len, LANES))
        for t in range(tiles):
            span = pl.ds(t * LANES, LANES)
            left, right = left_ref[:, span], right_ref[:, span]
            halos_ref[:, span] = right
            halos_ref[:, pl.ds((tiles + t) * LANES, LANES)] = left
            if t == 0:
                edge = jnp.where(lane < halo, right, jnp.where(lane >= LANES - halo, left, 0.0))
                wide_ref[:, pl.ds(height_len, LANES)] = edge
        wide_ref[:, pl.ds(0, height_len)] = column_ref[...]

    wide_column, halos = pl.pallas_call(
        widen_kernel,
        name="widen",
        compiler_params=GRANT,
        out_shape=(
            pltpu.VMEM((depth_len, wide), jnp.float32),
            pltpu.VMEM((depth_len, 2 * tiles * LANES), jnp.float32),
        ),
    )(*in_vmem(column, from_left, from_right))

    near = []
    for k in range(1, chain):
        near.append(lax.ppermute(wide_column, "light", light_pairs(k, chain)))

    gain_far, through_far = pl.pallas_call(
        gains_body,
        name="far_gains",
        compiler_params=GRANT,
        in_specs=[SMEM] * 2 + [VMEM],
        out_shape=gains_shape,
        scratch_shapes=gains_scratch,
    )(*in_smem(dirs, exts), *in_vmem(theirs))

    joined = (chain - 2) * depth_len

    def join_kernel(*refs):
        out_ref = refs[-1]
        for k, ref in enumerate(refs[: chain - 2]):
            out_ref[pl.ds(k * depth_len, depth_len), :] = ref[...]
        for t in range(2 * tiles):
            row, lane = divmod(t * LANES, wide)
            out_ref[pl.ds(joined + row * depth_len, depth_len), pl.ds(lane, LANES)] = refs[
                chain - 2
            ][:, pl.ds(t * LANES, LANES)]

    parcel = pl.pallas_call(
        join_kernel,
        name="join",
        compiler_params=GRANT,
        out_shape=pltpu.VMEM((joined + halo_rows, wide), jnp.float32),
    )(*in_vmem(*near[1:], halos))
    far_parcel = lax.ppermute(parcel, "depth", swap)
    far_last = lax.ppermute(near[0], "depth", swap)

    def chain_kernel(
        dir_ref, ext_ref, albedo_ref, lamp_ref, theirs_ref, near_last_ref, far_last_ref,
        near_ref, far_ref, taps_ref,
        gain_near_ref, through_near_ref, gain_far_ref, through_far_ref, out_ref, walls, plane, lit,
    ):
        light = lax.axis_index("light")
        depth = lax.axis_index("depth")
        height = lax.axis_index("height")
        own_row = pl.multiple_of(depth * depth_len, BZ)
        other_row = pl.multiple_of((1 - depth) * depth_len, BZ)
        for k in range(1, chain):
            source = peer(light, k, chain)
            for row, last, others in (
                (own_row, near_last_ref, near_ref),
                (other_row, far_last_ref, far_ref),
            ):
                if k > 1:
                    column = others[pl.ds((k - 2) * depth_len, depth_len), :]
                else:
                    column = last[...]
                walls[source, pl.ds(row, depth_len), :] = column
        lane = lane_iota((depth_len, LANES))

        def halo_tile(ref, t):
            row, first = divmod(t * LANES, wide)
            return ref[pl.ds(joined + row * depth_len, depth_len), pl.ds(first, LANES)]

        down = [dir_ref[depth * mine + i] for i in range(mine)]
        ups = mine - sum(down[1:], down[0])
        rank, ups_seen, downs_seen = [], 0, 0
        for i in range(mine):
            rank.append(jnp.where(down[i] == 1, ups + downs_seen, ups_seen))
            ups_seen = ups_seen + 1 - down[i]
            downs_seen = downs_seen + down[i]
        order = [
            sum((jnp.where(rank[i] == r, i, 0) for i in range(1, mine)), jnp.int32(0))
            for r in range(mine)
        ]
        for i in range(mine):
            for row, group, edges, body in (
                (own_row, 1 + i, near_ref, lamp_ref[depth * mine + i]),
                (other_row, 1 + mine + i, far_ref, theirs_ref[slices + i]),
            ):
                tile, shift = place(group)
                from_right = halo_tile(edges, tile)
                from_left = halo_tile(edges, tiles + tile)
                if shift:
                    from_right = pltpu.roll(from_right, LANES - shift, 1)
                    from_left = pltpu.roll(from_left, shift, 1)
                edge = jnp.where(
                    lane < halo, from_right, jnp.where(lane >= LANES - halo, from_left, 0.0)
                )
                plane[rank[i], pl.ds(row, depth_len), pl.ds(0, height_len)] = body
                plane[rank[i], pl.ds(row, depth_len), pl.ds(height_len, LANES)] = edge
        wide_lane = lane_iota((1, wide))
        inside = (
            (wide_lane < height_len)
            | ((wide_lane < height_len + LANES // 2) & (height < columns - 1))
            | ((wide_lane >= height_len + LANES // 2) & (height > 0))
        )
        inside = jnp.where(inside, 1.0, 0.0)
        ups_steps, down_steps = light, chain - 1 - light
        shared = jnp.minimum(ups_steps, down_steps)
        longest = jnp.maximum(ups_steps, down_steps)
        ups_longer = ups_steps > down_steps
        alone = jnp.where(ups_longer, ups, mine - ups)
        first_alone = jnp.where(ups_longer, 0, ups)
        as_pair = alone <= 2

        def advance(places, s):
            results = []
            for place_in in places:
                c = depth * mine + order[place_in] if isinstance(place_in, int) else None
                if c is None:
                    c = depth * mine + chosen(place_in)
                goes_down = place_in >= ups
                wall = walls[jnp.where(goes_down, chain - 1 - s, s)]
                before = plane[place_in]
                high, low = split(before * (jnp.exp(-ext_ref[c] * wall) * inside))
                bands = jnp.dot(
                    taps_ref[c - depth * mine],
                    jnp.concatenate([high, low, high], axis=0),
                    preferred_element_type=jnp.float32,
                )
                after = None
                for b in range(TAPS):
                    part = bands[b * full : (b + 1) * full]
                    if b != TAPS // 2:
                        part = pltpu.roll(part, (TAPS // 2 - b) % wide, 1)
                    after = part if after is None else after + part
                active = s < jnp.where(goes_down, down_steps, ups_steps)
                results.append(jnp.where(active, after, before))
            for place_in, after in zip(places, results):
                plane[place_in] = after

        def chosen(place_in):
            c = order[0]
            for i in range(1, mine):
                c = jnp.where(place_in == i, order[i], c)
            return c

        def all_step(s, carry):
            advance(range(mine), s)
            return carry

        def pair_step(s, carry):
            advance((first_alone, first_alone + jnp.maximum(alone - 1, 0)), s)
            return carry

        lax.fori_loop(0, jnp.where(as_pair, shared, longest), all_step, 0)
        lax.fori_loop(
            shared, jnp.where(as_pair & (alone > 0), longest, shared), pair_step, 0
        )
        in_front = depth == 0
        for i in range(mine):
            for half, row in enumerate((own_row, other_row)):
                lit[half, i] = plane[rank[i], pl.ds(row, depth_len), pl.ds(0, height_len)]
            shade = albedo_ref[depth * mine + i]
            sums = []
            for half, gain in enumerate((gain_near_ref, gain_far_ref)):
                parts = [None] * blocks
                for z in range(depth_len):
                    for j in range(blocks):
                        span = pl.ds(j * LANES, LANES)
                        part = lit[half, i, pl.ds(z, 1), span] * gain[i, z, :, span]
                        parts[j] = part if z == 0 else parts[j] + part
                sums.append(parts)
            for j in range(blocks):
                span = pl.ds(j * LANES, LANES)
                front = jnp.where(in_front, sums[0][j], sums[1][j])
                back = jnp.where(in_front, sums[1][j], sums[0][j])
                through = jnp.where(in_front, through_near_ref[:, span], through_far_ref[:, span])
                out_ref[i, :, span] = shade * (front + through * back)

    return pl.pallas_call(
        chain_kernel,
        name="chain",
        compiler_params=GRANT,
        in_specs=[SMEM] * 3 + [VMEM] * 11,
        out_specs=VMEM,
        out_shape=jax.ShapeDtypeStruct((mine, slices, height_len), jnp.float32),
        scratch_shapes=[
            pltpu.VMEM((chain, full, wide), jnp.float32),
            pltpu.VMEM((mine, full, wide), jnp.float32),
            pltpu.VMEM((groups, mine, depth_len, height_len), jnp.float32),
        ],
    )(
        *in_smem(dirs, exts, albedos),
        *in_vmem(lamp_plane, theirs, near[0], far_last, parcel, far_parcel, taps),
        *in_vmem(gain_near, through_near, gain_far, through_far),
    )


def solution(mesh):
    in_specs = (
        P("light", "depth", "height"),
        P("depth", None),
        P(),
        P(None, "depth", "height"),
        P(),
        P(),
        P(),
    )
    out_specs = P("depth", "light", "height")

    return jax.shard_map(local, mesh=mesh, in_specs=in_specs, out_specs=out_specs, check_vma=False)
```

```python
import jax
import jax.numpy as jnp
from jax import lax
from jax.experimental import pallas as pl
from jax.experimental.pallas import tpu as pltpu
from jax.sharding import PartitionSpec as P

BZ = 8
LANES = 128
TAPS = 5
GRANT = pltpu.CompilerParams(vmem_limit_bytes=24 << 20)
SMEM = pl.BlockSpec(memory_space=pltpu.SMEM)
VMEM = pl.BlockSpec(memory_space=pltpu.VMEM)
HBM = pl.BlockSpec(memory_space=pltpu.HBM)


def loops(lights, heights):
    steps = []
    for light in range(0, lights, 2):
        loop = [light * heights + h for h in range(heights)]
        loop += [(light + 1) * heights + h for h in reversed(range(heights))]
        steps += list(zip(loop, loop[1:] + loop[:1]))
    return steps


def peer(position, k, count):
    if count & (count - 1) == 0:
        return position ^ k
    return (position - k) % count


def light_pairs(k, count):
    return [(peer(i, k, count), i) for i in range(count)]


def lane_iota(shape):
    return lax.broadcasted_iota(jnp.int32, shape, len(shape) - 1)


def in_vmem(*values):
    return [pltpu.with_memory_space_constraint(v, pltpu.VMEM) for v in values]


def in_hbm(*values):
    return [pltpu.with_memory_space_constraint(v, pltpu.HBM) for v in values]


def in_smem(*values):
    return [pltpu.with_memory_space_constraint(v, pltpu.SMEM) for v in values]


def split(value):
    high = value.astype(jnp.bfloat16)
    return high, (value - high.astype(jnp.float32)).astype(jnp.bfloat16)


def local(density, active_list, light_dir, lamp_plane, extinction, blur_weights, albedo):
    colours = extinction.shape[0]
    slices, depth_len, height_len = density.shape
    chain = lax.axis_size("light")
    groups = lax.axis_size("depth")
    columns = lax.axis_size("height")
    assert groups == 2
    mine = colours // groups
    full = depth_len * groups
    halo = 2 * (chain - 1)
    assert 2 * halo <= LANES
    wide = height_len + LANES
    per_tile = LANES // halo
    tiles = -(-(1 + colours) // per_tile)
    assert 2 * tiles * LANES <= wide * chain
    blocks = height_len // LANES
    slabs = depth_len // BZ
    halo_rows = -(-2 * tiles * LANES // wide) * depth_len

    def place(g):
        return g // per_tile, (g % per_tile) * halo

    def sums_kernel(
        density_hbm, active_hbm, lamp_hbm, dir_hbm, ext_hbm, blur_hbm, albedo_hbm,
        cells_ref, column_ref, along_ref, against_ref, lamp_ref, dir_ref, ext_ref, blur_ref, albedo_ref,
        density_ref, active_ref, arrivals,
    ):
        light = lax.axis_index("light")
        depth = lax.axis_index("depth")
        height = lax.axis_index("height")
        moves = [
            pltpu.make_async_copy(source, target, arrivals.at[i])
            for i, (source, target) in enumerate(
                (
                    (active_hbm, active_ref),
                    (density_hbm, density_ref),
                    (lamp_hbm, lamp_ref),
                    (dir_hbm, dir_ref),
                    (ext_hbm, ext_ref),
                    (blur_hbm, blur_ref),
                    (albedo_hbm, albedo_ref),
                )
            )
        ]
        for move in moves:
            move.start()
        moves[0].wait()
        listed = active_ref[...]
        first_brick = (light * columns + height) * blocks
        lives = []
        for j in range(blocks):
            hit = jnp.max(
                jnp.where(listed == first_brick + j, 1.0, 0.0), axis=1, keepdims=True
            )
            lives.append(
                jnp.concatenate(
                    [jnp.broadcast_to(hit[r : r + 1], (BZ, LANES)) for r in range(slabs)], axis=0
                )
            )
        sums = [None] * blocks
        moves[1].wait()
        for x in range(slices):
            for j in range(blocks):
                span = pl.ds(j * LANES, LANES)
                cell = density_ref[x, :, span] * lives[j]
                cells_ref[x, :, span] = cell
                sums[j] = cell if x == 0 else sums[j] + cell
        for j in range(blocks):
            column_ref[:, pl.ds(j * LANES, LANES)] = sums[j]
        moves[2].wait()
        lane = lane_iota((depth_len, LANES))
        low = [jnp.zeros((depth_len, LANES), jnp.float32) for _ in range(tiles)]
        high = [jnp.zeros((depth_len, LANES), jnp.float32) for _ in range(tiles)]
        for g in range(1 + colours):
            tile, shift = place(g)
            if g == 0:
                left, right = sums[0], sums[-1]
            else:
                owner = depth if g <= mine else 1 - depth
                c = owner * mine + (g - 1) % mine
                left = lamp_ref[c, :, pl.ds(0, LANES)]
                right = lamp_ref[c, :, pl.ds(height_len - LANES, LANES)]
            if shift:
                left = pltpu.roll(left, shift, 1)
                right = pltpu.roll(right, LANES - shift, 1)
            low[tile] = jnp.where((lane >= shift) & (lane < shift + halo), left, low[tile])
            high[tile] = jnp.where(
                (lane >= LANES - shift - halo) & (lane < LANES - shift), right, high[tile]
            )
        upwards = light % 2 == 0
        for t in range(tiles):
            span = pl.ds(t * LANES, LANES)
            along_ref[:, span] = jnp.where(upwards, high[t], low[t])
            against_ref[:, span] = jnp.where(upwards, low[t], high[t])
        for move in moves[3:]:
            move.wait()

    cells, column, edge_along, edge_against, lamps, dirs, exts, blurs, albedos = pl.pallas_call(
        sums_kernel,
        name="sums",
        compiler_params=GRANT,
        in_specs=[HBM] * 7,
        out_specs=[VMEM] * 5 + [SMEM] * 4,
        out_shape=(
            pltpu.VMEM(density.shape, jnp.float32),
            pltpu.VMEM((depth_len, height_len), jnp.float32),
            pltpu.VMEM((depth_len, tiles * LANES), jnp.float32),
            pltpu.VMEM((depth_len, tiles * LANES), jnp.float32),
            pltpu.VMEM(lamp_plane.shape, jnp.float32),
            pltpu.SMEM(light_dir.shape, jnp.int32),
            pltpu.SMEM(extinction.shape, jnp.float32),
            pltpu.SMEM(blur_weights.shape, jnp.float32),
            pltpu.SMEM(albedo.shape, jnp.float32),
        ),
        scratch_shapes=[
            pltpu.VMEM(density.shape, jnp.float32),
            pltpu.VMEM(active_list.shape, jnp.int32),
            pltpu.SemaphoreType.DMA((7,)),
        ],
    )(*in_hbm(density, active_list, lamp_plane, light_dir, extinction, blur_weights, albedo))

    swap = [(0, 1), (1, 0)]
    assert chain % 2 == 0
    along = loops(chain, columns)
    got_along = lax.ppermute(edge_along, ("light", "height"), along)
    got_against = lax.ppermute(
        edge_against, ("light", "height"), [(target, source) for source, target in along]
    )

    def gains_body(dir_ref, ext_ref, cells_ref, gain_ref, through_ref, cells, earlier):
        depth = lax.axis_index("depth")
        for j in range(blocks):
            running = jnp.zeros((depth_len, LANES), jnp.float32)
            for x in range(slices):
                rows = pl.ds(x * depth_len, depth_len)
                cell = cells_ref[x, :, pl.ds(j * LANES, LANES)]
                cells[j, rows, :] = cell
                earlier[j, rows, :] = running
                running = running + cell
            earlier[j, pl.ds(slices * depth_len, depth_len), :] = running
        down = [dir_ref[depth * mine + i] == 1 for i in range(mine)]
        rate = [-ext_ref[depth * mine + i] for i in range(mine)]

        def one_depth(z, through):
            passed = []
            for j in range(blocks):
                span = pl.ds(j * LANES, LANES)
                cell = cells[j, pl.ds(z, slices, stride=depth_len), :]
                before_up = earlier[j, pl.ds(z, slices, stride=depth_len), :]
                total = earlier[j, pl.ds(slices * depth_len + z, 1), :]
                before_down = total - before_up - cell
                kept = jnp.exp(cell * (-6.0 / full))
                weight = through[j] * (1.0 - kept)
                for i in range(mine):
                    before = jnp.where(down[i], before_down, before_up)
                    gain_ref[i, z, :, span] = weight * jnp.exp(rate[i] * before)
                passed.append(through[j] * kept)
            return tuple(passed)

        start = tuple(jnp.ones((slices, LANES), jnp.float32) for _ in range(blocks))
        for j, value in enumerate(lax.fori_loop(0, depth_len, one_depth, start)):
            through_ref[:, pl.ds(j * LANES, LANES)] = value

    gains_shape = (
        pltpu.VMEM((mine, depth_len, slices, height_len), jnp.float32),
        pltpu.VMEM((slices, height_len), jnp.float32),
    )
    gains_scratch = [
        pltpu.VMEM((blocks, slices * depth_len, LANES), jnp.float32),
        pltpu.VMEM((blocks, (slices + 1) * depth_len, LANES), jnp.float32),
    ]

    def near_kernel(
        dir_ref, ext_ref, blur_ref, cells_ref, lamp_ref, gain_ref, through_ref, taps_ref, bundle_ref,
        *scratch,
    ):
        depth = lax.axis_index("depth")
        shape = (full, LANES)
        lane = lane_iota(shape)
        offset = lane % full - lax.broadcasted_iota(jnp.int32, shape, 0) + TAPS // 2
        for i in range(mine):
            c = depth * mine + i
            norm = blur_ref[c, 0]
            for tap in range(1, TAPS * TAPS):
                norm = norm + blur_ref[c, tap]
            inverse = 1.0 / jnp.full(shape, norm, jnp.float32)
            for b in range(TAPS):
                band = jnp.zeros(shape, jnp.float32)
                for a in range(TAPS):
                    band = jnp.where(offset == a, blur_ref[c, a * TAPS + b], band)
                band = band * inverse
                high = band.astype(jnp.bfloat16).astype(jnp.float32)
                band = jnp.where(lane < 2 * full, high, band - high)
                taps_ref[i, pl.ds(b * full, full), :] = band.astype(jnp.bfloat16)[:, : 3 * full]
        for x in range(slices):
            bundle_ref[x] = cells_ref[x]
        for i in range(mine):
            bundle_ref[slices + i] = lamp_ref[(1 - depth) * mine + i]
        gains_body(dir_ref, ext_ref, cells_ref, gain_ref, through_ref, *scratch)

    gain_near, through_near, taps, bundle = pl.pallas_call(
        near_kernel,
        name="near_gains",
        compiler_params=GRANT,
        in_specs=[SMEM] * 3 + [VMEM] * 2,
        out_shape=gains_shape
        + (
            pltpu.VMEM((mine, TAPS * full, 3 * full), jnp.bfloat16),
            pltpu.VMEM((slices + mine, depth_len, height_len), jnp.float32),
        ),
        scratch_shapes=gains_scratch,
    )(*in_smem(dirs, exts, blurs), *in_vmem(cells, lamps))

    theirs = lax.ppermute(bundle, "depth", swap)

    def widen_kernel(column_ref, along_ref, against_ref, wide_ref, halos_ref):
        upwards = lax.axis_index("light") % 2 == 0
        lane = lane_iota((depth_len, LANES))
        for t in range(tiles):
            span = pl.ds(t * LANES, LANES)
            along, against = along_ref[:, span], against_ref[:, span]
            left = jnp.where(upwards, along, against)
            right = jnp.where(upwards, against, along)
            halos_ref[:, span] = right
            halos_ref[:, pl.ds((tiles + t) * LANES, LANES)] = left
            if t == 0:
                edge = jnp.where(lane < halo, right, jnp.where(lane >= LANES - halo, left, 0.0))
                wide_ref[:, pl.ds(height_len, LANES)] = edge
        wide_ref[:, pl.ds(0, height_len)] = column_ref[...]

    wide_column, halos = pl.pallas_call(
        widen_kernel,
        name="widen",
        compiler_params=GRANT,
        out_shape=(
            pltpu.VMEM((depth_len, wide), jnp.float32),
            pltpu.VMEM((depth_len, 2 * tiles * LANES), jnp.float32),
        ),
    )(*in_vmem(column, got_along, got_against))

    near = []
    for k in range(1, chain):
        near.append(lax.ppermute(wide_column, "light", light_pairs(k, chain)))

    gain_far, through_far = pl.pallas_call(
        gains_body,
        name="far_gains",
        compiler_params=GRANT,
        in_specs=[SMEM] * 2 + [VMEM],
        out_shape=gains_shape,
        scratch_shapes=gains_scratch,
    )(*in_smem(dirs, exts), *in_vmem(theirs))

    joined = (chain - 2) * depth_len

    def join_kernel(*refs):
        out_ref = refs[-1]
        for k, ref in enumerate(refs[: chain - 2]):
            out_ref[pl.ds(k * depth_len, depth_len), :] = ref[...]
        for t in range(2 * tiles):
            row, lane = divmod(t * LANES, wide)
            out_ref[pl.ds(joined + row * depth_len, depth_len), pl.ds(lane, LANES)] = refs[
                chain - 2
            ][:, pl.ds(t * LANES, LANES)]

    parcel = pl.pallas_call(
        join_kernel,
        name="join",
        compiler_params=GRANT,
        out_shape=pltpu.VMEM((joined + halo_rows, wide), jnp.float32),
    )(*in_vmem(*near[1:], halos))
    far_parcel = lax.ppermute(parcel, "depth", swap)
    far_last = lax.ppermute(near[0], "depth", swap)

    def chain_kernel(
        dir_ref, ext_ref, albedo_ref, lamp_ref, theirs_ref, near_last_ref, far_last_ref,
        near_ref, far_ref, taps_ref,
        gain_near_ref, through_near_ref, gain_far_ref, through_far_ref, out_ref, walls, plane, lit,
    ):
        light = lax.axis_index("light")
        depth = lax.axis_index("depth")
        height = lax.axis_index("height")
        own_row = pl.multiple_of(depth * depth_len, BZ)
        other_row = pl.multiple_of((1 - depth) * depth_len, BZ)
        for k in range(1, chain):
            source = peer(light, k, chain)
            for row, last, others in (
                (own_row, near_last_ref, near_ref),
                (other_row, far_last_ref, far_ref),
            ):
                if k > 1:
                    column = others[pl.ds((k - 2) * depth_len, depth_len), :]
                else:
                    column = last[...]
                walls[source, pl.ds(row, depth_len), :] = column
        lane = lane_iota((depth_len, LANES))

        def halo_tile(ref, t):
            row, first = divmod(t * LANES, wide)
            return ref[pl.ds(joined + row * depth_len, depth_len), pl.ds(first, LANES)]

        down = [dir_ref[depth * mine + i] for i in range(mine)]
        ups = mine - sum(down[1:], down[0])
        rank, ups_seen, downs_seen = [], 0, 0
        for i in range(mine):
            rank.append(jnp.where(down[i] == 1, ups + downs_seen, ups_seen))
            ups_seen = ups_seen + 1 - down[i]
            downs_seen = downs_seen + down[i]
        order = [
            sum((jnp.where(rank[i] == r, i, 0) for i in range(1, mine)), jnp.int32(0))
            for r in range(mine)
        ]
        for i in range(mine):
            for row, group, edges, body in (
                (own_row, 1 + i, near_ref, lamp_ref[depth * mine + i]),
                (other_row, 1 + mine + i, far_ref, theirs_ref[slices + i]),
            ):
                tile, shift = place(group)
                from_right = halo_tile(edges, tile)
                from_left = halo_tile(edges, tiles + tile)
                if shift:
                    from_right = pltpu.roll(from_right, LANES - shift, 1)
                    from_left = pltpu.roll(from_left, shift, 1)
                edge = jnp.where(
                    lane < halo, from_right, jnp.where(lane >= LANES - halo, from_left, 0.0)
                )
                plane[rank[i], pl.ds(row, depth_len), pl.ds(0, height_len)] = body
                plane[rank[i], pl.ds(row, depth_len), pl.ds(height_len, LANES)] = edge
        wide_lane = lane_iota((1, wide))
        inside = (
            (wide_lane < height_len)
            | ((wide_lane < height_len + LANES // 2) & (height < columns - 1))
            | ((wide_lane >= height_len + LANES // 2) & (height > 0))
        )
        inside = jnp.where(inside, 1.0, 0.0)
        ups_steps, down_steps = light, chain - 1 - light
        shared = jnp.minimum(ups_steps, down_steps)
        longest = jnp.maximum(ups_steps, down_steps)
        ups_longer = ups_steps > down_steps
        alone = jnp.where(ups_longer, ups, mine - ups)
        first_alone = jnp.where(ups_longer, 0, ups)
        as_pair = alone <= 2

        def advance(places, s):
            results = []
            for place_in in places:
                c = depth * mine + order[place_in] if isinstance(place_in, int) else None
                if c is None:
                    c = depth * mine + chosen(place_in)
                goes_down = place_in >= ups
                wall = walls[jnp.where(goes_down, chain - 1 - s, s)]
                before = plane[place_in]
                high, low = split(before * (jnp.exp(-ext_ref[c] * wall) * inside))
                bands = jnp.dot(
                    taps_ref[c - depth * mine],
                    jnp.concatenate([high, low, high], axis=0),
                    preferred_element_type=jnp.float32,
                )
                after = None
                for b in range(TAPS):
                    part = bands[b * full : (b + 1) * full]
                    if b != TAPS // 2:
                        part = pltpu.roll(part, (TAPS // 2 - b) % wide, 1)
                    after = part if after is None else after + part
                active = s < jnp.where(goes_down, down_steps, ups_steps)
                results.append(jnp.where(active, after, before))
            for place_in, after in zip(places, results):
                plane[place_in] = after

        def chosen(place_in):
            c = order[0]
            for i in range(1, mine):
                c = jnp.where(place_in == i, order[i], c)
            return c

        def all_step(s, carry):
            advance(range(mine), s)
            return carry

        def pair_step(s, carry):
            advance((first_alone, first_alone + jnp.maximum(alone - 1, 0)), s)
            return carry

        lax.fori_loop(0, jnp.where(as_pair, shared, longest), all_step, 0)
        lax.fori_loop(
            shared, jnp.where(as_pair & (alone > 0), longest, shared), pair_step, 0
        )
        in_front = depth == 0
        for i in range(mine):
            for half, row in enumerate((own_row, other_row)):
                lit[half, i] = plane[rank[i], pl.ds(row, depth_len), pl.ds(0, height_len)]
            shade = albedo_ref[depth * mine + i]
            sums = []
            for half, gain in enumerate((gain_near_ref, gain_far_ref)):
                parts = [None] * blocks
                for z in range(depth_len):
                    for j in range(blocks):
                        span = pl.ds(j * LANES, LANES)
                        part = lit[half, i, pl.ds(z, 1), span] * gain[i, z, :, span]
                        parts[j] = part if z == 0 else parts[j] + part
                sums.append(parts)
            for j in range(blocks):
                span = pl.ds(j * LANES, LANES)
                front = jnp.where(in_front, sums[0][j], sums[1][j])
                back = jnp.where(in_front, sums[1][j], sums[0][j])
                through = jnp.where(in_front, through_near_ref[:, span], through_far_ref[:, span])
                out_ref[i, :, span] = shade * (front + through * back)

    return pl.pallas_call(
        chain_kernel,
        name="chain",
        compiler_params=GRANT,
        in_specs=[SMEM] * 3 + [VMEM] * 11,
        out_specs=VMEM,
        out_shape=jax.ShapeDtypeStruct((mine, slices, height_len), jnp.float32),
        scratch_shapes=[
            pltpu.VMEM((chain, full, wide), jnp.float32),
            pltpu.VMEM((mine, full, wide), jnp.float32),
            pltpu.VMEM((groups, mine, depth_len, height_len), jnp.float32),
        ],
    )(
        *in_smem(dirs, exts, albedos),
        *in_vmem(lamps, theirs, near[0], far_last, parcel, far_parcel, taps),
        *in_vmem(gain_near, through_near, gain_far, through_far),
    )


def solution(mesh):
    in_specs = (
        P("light", "depth", "height"),
        P("depth", None),
        P(),
        P(None, "depth", "height"),
        P(),
        P(),
        P(),
    )
    out_specs = P("depth", "light", "height")

    return jax.shard_map(local, mesh=mesh, in_specs=in_specs, out_specs=out_specs, check_vma=False)
```

```python
import jax
import jax.numpy as jnp
from jax import lax
from jax.experimental import pallas as pl
from jax.experimental.pallas import tpu as pltpu
from jax.sharding import PartitionSpec as P

BZ = 8
LANES = 128
TAPS = 5
GRANT = pltpu.CompilerParams(vmem_limit_bytes=24 << 20)
SMEM = pl.BlockSpec(memory_space=pltpu.SMEM)
VMEM = pl.BlockSpec(memory_space=pltpu.VMEM)
HBM = pl.BlockSpec(memory_space=pltpu.HBM)


def loops(lights, heights):
    steps = []
    for light in range(0, lights, 2):
        loop = [light * heights + h for h in range(heights)]
        loop += [(light + 1) * heights + h for h in reversed(range(heights))]
        steps += list(zip(loop, loop[1:] + loop[:1]))
    return steps


def peer(position, k):
    return position ^ k


def light_pairs(k, count):
    return [(peer(i, k), i) for i in range(count)]


def lane_iota(shape):
    return lax.broadcasted_iota(jnp.int32, shape, len(shape) - 1)


def in_vmem(*values):
    return [pltpu.with_memory_space_constraint(v, pltpu.VMEM) for v in values]


def in_hbm(*values):
    return [pltpu.with_memory_space_constraint(v, pltpu.HBM) for v in values]


def in_smem(*values):
    return [pltpu.with_memory_space_constraint(v, pltpu.SMEM) for v in values]


def split(value):
    high = value.astype(jnp.bfloat16)
    return high, (value - high.astype(jnp.float32)).astype(jnp.bfloat16)


def local(density, active_list, light_dir, lamp_plane, extinction, blur_weights, albedo):
    colours = extinction.shape[0]
    slices, depth_len, height_len = density.shape
    chain = lax.axis_size("light")
    groups = lax.axis_size("depth")
    columns = lax.axis_size("height")
    assert groups == 2
    mine = colours // groups
    full = depth_len * groups
    halo = 2 * (chain - 1)
    assert 2 * halo <= LANES
    wide = height_len + LANES
    per_tile = LANES // halo
    tiles = -(-(1 + colours) // per_tile)
    assert 2 * tiles * LANES <= wide * chain
    blocks = height_len // LANES
    slabs = depth_len // BZ
    halo_rows = -(-2 * tiles * LANES // wide) * depth_len

    def place(g):
        return g // per_tile, (g % per_tile) * halo

    def sums_kernel(
        density_hbm, active_hbm, lamp_hbm, dir_hbm, ext_hbm, blur_hbm, albedo_hbm,
        cells_ref, column_ref, along_ref, against_ref, lamp_ref, dir_ref, ext_ref, blur_ref, albedo_ref,
        density_ref, active_ref, arrivals,
    ):
        light = lax.axis_index("light")
        depth = lax.axis_index("depth")
        height = lax.axis_index("height")
        moves = [
            pltpu.make_async_copy(source, target, arrivals.at[i])
            for i, (source, target) in enumerate(
                (
                    (active_hbm, active_ref),
                    (density_hbm, density_ref),
                    (lamp_hbm, lamp_ref),
                    (dir_hbm, dir_ref),
                    (ext_hbm, ext_ref),
                    (blur_hbm, blur_ref),
                    (albedo_hbm, albedo_ref),
                )
            )
        ]
        for move in moves:
            move.start()
        moves[0].wait()
        listed = active_ref[...]
        first_brick = (light * columns + height) * blocks
        lives = []
        for j in range(blocks):
            hit = jnp.max(
                jnp.where(listed == first_brick + j, 1.0, 0.0), axis=1, keepdims=True
            )
            lives.append(
                jnp.concatenate(
                    [jnp.broadcast_to(hit[r : r + 1], (BZ, LANES)) for r in range(slabs)], axis=0
                )
            )
        sums = [None] * blocks
        moves[1].wait()
        for x in range(slices):
            for j in range(blocks):
                span = pl.ds(j * LANES, LANES)
                cell = density_ref[x, :, span] * lives[j]
                cells_ref[x, :, span] = cell
                sums[j] = cell if x == 0 else sums[j] + cell
        for j in range(blocks):
            column_ref[:, pl.ds(j * LANES, LANES)] = sums[j]
        moves[2].wait()
        lane = lane_iota((depth_len, LANES))
        low = [jnp.zeros((depth_len, LANES), jnp.float32) for _ in range(tiles)]
        high = [jnp.zeros((depth_len, LANES), jnp.float32) for _ in range(tiles)]
        for g in range(1 + colours):
            tile, shift = place(g)
            if g == 0:
                left, right = sums[0], sums[-1]
            else:
                owner = depth if g <= mine else 1 - depth
                c = owner * mine + (g - 1) % mine
                left = lamp_ref[c, :, pl.ds(0, LANES)]
                right = lamp_ref[c, :, pl.ds(height_len - LANES, LANES)]
            if shift:
                left = pltpu.roll(left, shift, 1)
                right = pltpu.roll(right, LANES - shift, 1)
            low[tile] = jnp.where((lane >= shift) & (lane < shift + halo), left, low[tile])
            high[tile] = jnp.where(
                (lane >= LANES - shift - halo) & (lane < LANES - shift), right, high[tile]
            )
        upwards = light % 2 == 0
        for t in range(tiles):
            span = pl.ds(t * LANES, LANES)
            along_ref[:, span] = jnp.where(upwards, high[t], low[t])
            against_ref[:, span] = jnp.where(upwards, low[t], high[t])
        for move in moves[3:]:
            move.wait()

    cells, column, edge_along, edge_against, lamps, dirs, exts, blurs, albedos = pl.pallas_call(
        sums_kernel,
        name="sums",
        compiler_params=GRANT,
        in_specs=[HBM] * 7,
        out_specs=[VMEM] * 5 + [SMEM] * 4,
        out_shape=(
            pltpu.VMEM(density.shape, jnp.float32),
            pltpu.VMEM((depth_len, height_len), jnp.float32),
            pltpu.VMEM((depth_len, tiles * LANES), jnp.float32),
            pltpu.VMEM((depth_len, tiles * LANES), jnp.float32),
            pltpu.VMEM(lamp_plane.shape, jnp.float32),
            pltpu.SMEM(light_dir.shape, jnp.int32),
            pltpu.SMEM(extinction.shape, jnp.float32),
            pltpu.SMEM(blur_weights.shape, jnp.float32),
            pltpu.SMEM(albedo.shape, jnp.float32),
        ),
        scratch_shapes=[
            pltpu.VMEM(density.shape, jnp.float32),
            pltpu.VMEM(active_list.shape, jnp.int32),
            pltpu.SemaphoreType.DMA((7,)),
        ],
    )(*in_hbm(density, active_list, lamp_plane, light_dir, extinction, blur_weights, albedo))

    swap = [(0, 1), (1, 0)]
    assert chain & (chain - 1) == 0 and chain > 2
    along = loops(chain, columns)
    got_along = lax.ppermute(edge_along, ("light", "height"), along)
    got_against = lax.ppermute(
        edge_against, ("light", "height"), [(target, source) for source, target in along]
    )

    def gains_body(dir_ref, ext_ref, cells_ref, gain_ref, through_ref, cells, earlier):
        depth = lax.axis_index("depth")
        for j in range(blocks):
            running = jnp.zeros((depth_len, LANES), jnp.float32)
            for x in range(slices):
                rows = pl.ds(x * depth_len, depth_len)
                cell = cells_ref[x, :, pl.ds(j * LANES, LANES)]
                cells[j, rows, :] = cell
                earlier[j, rows, :] = running
                running = running + cell
            earlier[j, pl.ds(slices * depth_len, depth_len), :] = running
        down = [dir_ref[depth * mine + i] == 1 for i in range(mine)]
        rate = [-ext_ref[depth * mine + i] for i in range(mine)]

        def one_depth(z, through):
            passed = []
            for j in range(blocks):
                span = pl.ds(j * LANES, LANES)
                cell = cells[j, pl.ds(z, slices, stride=depth_len), :]
                before_up = earlier[j, pl.ds(z, slices, stride=depth_len), :]
                total = earlier[j, pl.ds(slices * depth_len + z, 1), :]
                before_down = total - before_up - cell
                kept = jnp.exp(cell * (-6.0 / full))
                weight = through[j] * (1.0 - kept)
                for i in range(mine):
                    before = jnp.where(down[i], before_down, before_up)
                    gain_ref[i, z, :, span] = weight * jnp.exp(rate[i] * before)
                passed.append(through[j] * kept)
            return tuple(passed)

        start = tuple(jnp.ones((slices, LANES), jnp.float32) for _ in range(blocks))
        for j, value in enumerate(lax.fori_loop(0, depth_len, one_depth, start)):
            through_ref[:, pl.ds(j * LANES, LANES)] = value

    gains_shape = (
        pltpu.VMEM((mine, depth_len, slices, height_len), jnp.float32),
        pltpu.VMEM((slices, height_len), jnp.float32),
    )
    gains_scratch = [
        pltpu.VMEM((blocks, slices * depth_len, LANES), jnp.float32),
        pltpu.VMEM((blocks, (slices + 1) * depth_len, LANES), jnp.float32),
    ]

    def near_kernel(
        dir_ref, ext_ref, blur_ref, cells_ref, lamp_ref, gain_ref, through_ref, taps_ref, bundle_ref,
        *scratch,
    ):
        depth = lax.axis_index("depth")
        shape = (full, LANES)
        lane = lane_iota(shape)
        offset = lane % full - lax.broadcasted_iota(jnp.int32, shape, 0) + TAPS // 2
        for i in range(mine):
            c = depth * mine + i
            norm = blur_ref[c, 0]
            for tap in range(1, TAPS * TAPS):
                norm = norm + blur_ref[c, tap]
            inverse = 1.0 / jnp.full(shape, norm, jnp.float32)
            for b in range(TAPS):
                band = jnp.zeros(shape, jnp.float32)
                for a in range(TAPS):
                    band = jnp.where(offset == a, blur_ref[c, a * TAPS + b], band)
                band = band * inverse
                high = band.astype(jnp.bfloat16).astype(jnp.float32)
                band = jnp.where(lane < 2 * full, high, band - high)
                taps_ref[i, pl.ds(b * full, full), :] = band.astype(jnp.bfloat16)[:, : 3 * full]
        for x in range(slices):
            bundle_ref[x] = cells_ref[x]
        for i in range(mine):
            bundle_ref[slices + i] = lamp_ref[(1 - depth) * mine + i]
        gains_body(dir_ref, ext_ref, cells_ref, gain_ref, through_ref, *scratch)

    gain_near, through_near, taps, bundle = pl.pallas_call(
        near_kernel,
        name="near_gains",
        compiler_params=GRANT,
        in_specs=[SMEM] * 3 + [VMEM] * 2,
        out_shape=gains_shape
        + (
            pltpu.VMEM((mine, TAPS * full, 3 * full), jnp.bfloat16),
            pltpu.VMEM((slices + mine, depth_len, height_len), jnp.float32),
        ),
        scratch_shapes=gains_scratch,
    )(*in_smem(dirs, exts, blurs), *in_vmem(cells, lamps))

    theirs = lax.ppermute(bundle, "depth", swap)

    def widen_kernel(column_ref, along_ref, against_ref, wide_ref, halos_ref):
        upwards = lax.axis_index("light") % 2 == 0
        lane = lane_iota((depth_len, LANES))
        for t in range(tiles):
            span = pl.ds(t * LANES, LANES)
            along, against = along_ref[:, span], against_ref[:, span]
            left = jnp.where(upwards, along, against)
            right = jnp.where(upwards, against, along)
            halos_ref[:, span] = right
            halos_ref[:, pl.ds((tiles + t) * LANES, LANES)] = left
            if t == 0:
                edge = jnp.where(lane < halo, right, jnp.where(lane >= LANES - halo, left, 0.0))
                wide_ref[:, pl.ds(height_len, LANES)] = edge
        wide_ref[:, pl.ds(0, height_len)] = column_ref[...]

    wide_column, halos = pl.pallas_call(
        widen_kernel,
        name="widen",
        compiler_params=GRANT,
        out_shape=(
            pltpu.VMEM((depth_len, wide), jnp.float32),
            pltpu.VMEM((depth_len, 2 * tiles * LANES), jnp.float32),
        ),
    )(*in_vmem(column, got_along, got_against))

    near = []
    for k in range(1, chain):
        near.append(lax.ppermute(wide_column, "light", light_pairs(k, chain)))

    gain_far, through_far = pl.pallas_call(
        gains_body,
        name="far_gains",
        compiler_params=GRANT,
        in_specs=[SMEM] * 2 + [VMEM],
        out_shape=gains_shape,
        scratch_shapes=gains_scratch,
    )(*in_smem(dirs, exts), *in_vmem(theirs))

    joined = (chain - 3) * depth_len

    def join_kernel(*refs):
        out_ref = refs[-1]
        for k, ref in enumerate(refs[: chain - 3]):
            out_ref[pl.ds(k * depth_len, depth_len), :] = ref[...]
        for t in range(2 * tiles):
            row, lane = divmod(t * LANES, wide)
            out_ref[pl.ds(joined + row * depth_len, depth_len), pl.ds(lane, LANES)] = refs[
                chain - 3
            ][:, pl.ds(t * LANES, LANES)]

    parcel = pl.pallas_call(
        join_kernel,
        name="join",
        compiler_params=GRANT,
        out_shape=pltpu.VMEM((joined + halo_rows, wide), jnp.float32),
    )(*in_vmem(*near[2:], halos))
    far_parcel = lax.ppermute(parcel, "depth", swap)
    far_side = lax.ppermute(near[1], "depth", swap)
    far_last = lax.ppermute(near[0], "depth", swap)

    def sorted_colours(dir_ref, depth):
        down = [dir_ref[depth * mine + i] for i in range(mine)]
        ups = mine - sum(down[1:], down[0])
        rank, ups_seen, downs_seen = [], 0, 0
        for i in range(mine):
            rank.append(jnp.where(down[i] == 1, ups + downs_seen, ups_seen))
            ups_seen = ups_seen + 1 - down[i]
            downs_seen = downs_seen + down[i]
        order = [
            sum((jnp.where(rank[i] == r, i, 0) for i in range(1, mine)), jnp.int32(0))
            for r in range(mine)
        ]

        def colour(at):
            if isinstance(at, int):
                return order[at]
            c = order[0]
            for i in range(1, mine):
                c = jnp.where(at == i, order[i], c)
            return c

        return ups, rank, colour

    def inside_lanes():
        height = lax.axis_index("height")
        wide_lane = lane_iota((1, wide))
        inside = (
            (wide_lane < height_len)
            | ((wide_lane < height_len + LANES // 2) & (height < columns - 1))
            | ((wide_lane >= height_len + LANES // 2) & (height > 0))
        )
        return jnp.where(inside, 1.0, 0.0)

    def blurred(before, wall, rate, inside, taps):
        high, low = split(before * (jnp.exp(-rate * wall) * inside))
        bands = jnp.dot(
            taps, jnp.concatenate([high, low, high], axis=0), preferred_element_type=jnp.float32
        )
        after = None
        for b in range(TAPS):
            part = bands[b * full : (b + 1) * full]
            if b != TAPS // 2:
                part = pltpu.roll(part, (TAPS // 2 - b) % wide, 1)
            after = part if after is None else after + part
        return after

    def before_sides(length):
        return length - length % 4 + jnp.where(length % 4 == 3, 1, 0)

    def early_kernel(
        dir_ref, ext_ref, lamp_ref, theirs_ref, near_ref, far_ref, taps_ref, plane, walls,
    ):
        light = lax.axis_index("light")
        depth = lax.axis_index("depth")
        own_row = pl.multiple_of(depth * depth_len, BZ)
        other_row = pl.multiple_of((1 - depth) * depth_len, BZ)
        for k in range(3, chain):
            for row, ref in ((own_row, near_ref), (other_row, far_ref)):
                column = ref[pl.ds((k - 3) * depth_len, depth_len), :]
                walls[peer(light, k), pl.ds(row, depth_len), :] = column
        lane = lane_iota((depth_len, LANES))

        def halo_tile(ref, t):
            row, first = divmod(t * LANES, wide)
            return ref[pl.ds(joined + row * depth_len, depth_len), pl.ds(first, LANES)]

        ups, rank, colour = sorted_colours(dir_ref, depth)
        for i in range(mine):
            for row, group, edges, body in (
                (own_row, 1 + i, near_ref, lamp_ref[depth * mine + i]),
                (other_row, 1 + mine + i, far_ref, theirs_ref[slices + i]),
            ):
                tile, shift = place(group)
                from_right = halo_tile(edges, tile)
                from_left = halo_tile(edges, tiles + tile)
                if shift:
                    from_right = pltpu.roll(from_right, LANES - shift, 1)
                    from_left = pltpu.roll(from_left, shift, 1)
                edge = jnp.where(
                    lane < halo, from_right, jnp.where(lane >= LANES - halo, from_left, 0.0)
                )
                plane[rank[i], pl.ds(row, depth_len), pl.ds(0, height_len)] = body
                plane[rank[i], pl.ds(row, depth_len), pl.ds(height_len, LANES)] = edge
        inside = inside_lanes()
        ups_steps = before_sides(light)
        down_steps = before_sides(chain - 1 - light)
        shared = jnp.minimum(ups_steps, down_steps)
        longest = jnp.maximum(ups_steps, down_steps)
        ups_longer = ups_steps > down_steps
        alone = jnp.where(ups_longer, ups, mine - ups)
        first_alone = jnp.where(ups_longer, 0, ups)
        as_pair = alone <= 2

        def advance(places, s):
            results = []
            for at in places:
                c = colour(at)
                goes_down = at >= ups
                wall = walls[jnp.where(goes_down, chain - 1 - s, s)]
                before = plane[at]
                after = blurred(before, wall, ext_ref[depth * mine + c], inside, taps_ref[c])
                active = s < jnp.where(goes_down, down_steps, ups_steps)
                results.append(jnp.where(active, after, before))
            for at, after in zip(places, results):
                plane[at] = after

        def all_step(s, carry):
            advance(range(mine), s)
            return carry

        def pair_step(s, carry):
            advance((first_alone, first_alone + jnp.maximum(alone - 1, 0)), s)
            return carry

        lax.fori_loop(0, jnp.where(as_pair, shared, longest), all_step, 0)
        lax.fori_loop(shared, jnp.where(as_pair & (alone > 0), longest, shared), pair_step, 0)

    planes = pl.pallas_call(
        early_kernel,
        name="early",
        compiler_params=GRANT,
        in_specs=[SMEM] * 2 + [VMEM] * 5,
        out_shape=pltpu.VMEM((mine, full, wide), jnp.float32),
        scratch_shapes=[pltpu.VMEM((chain, full, wide), jnp.float32)],
    )(*in_smem(dirs, exts), *in_vmem(lamps, theirs, parcel, far_parcel, taps))

    def middle_kernel(
        dir_ref, ext_ref, planes_ref, near_ref, far_ref, side_ref, far_side_ref, taps_ref, plane, walls,
    ):
        light = lax.axis_index("light")
        depth = lax.axis_index("depth")
        own_row = pl.multiple_of(depth * depth_len, BZ)
        other_row = pl.multiple_of((1 - depth) * depth_len, BZ)
        walls[0, pl.ds(own_row, depth_len), :] = side_ref[...]
        walls[0, pl.ds(other_row, depth_len), :] = far_side_ref[...]
        walls[1, pl.ds(own_row, depth_len), :] = near_ref[pl.ds(0, depth_len), :]
        walls[1, pl.ds(other_row, depth_len), :] = far_ref[pl.ds(0, depth_len), :]
        ups, _, colour = sorted_colours(dir_ref, depth)
        inside = inside_lanes()
        ups_move = light % 4 >= 2
        length = jnp.where(ups_move, light, chain - 1 - light)
        start = before_sides(length)
        end = length - length % 2
        moving = jnp.where(ups_move, ups, mine - ups)
        first = jnp.where(ups_move, 0, ups)
        for i in range(mine):
            plane[i] = planes_ref[i]

        def advance(places, s):
            source = jnp.where(ups_move, s, chain - 1 - s)
            wall = walls[peer(light, source) - 2]
            results = []
            for at in places:
                c = colour(at)
                before = plane[at]
                after = blurred(before, wall, ext_ref[depth * mine + c], inside, taps_ref[c])
                moves = (at >= first) & (at < first + moving)
                results.append(jnp.where(moves, after, before))
            for at, after in zip(places, results):
                plane[at] = after

        def all_step(s, carry):
            advance(range(mine), s)
            return carry

        def pair_step(s, carry):
            advance((first, first + jnp.maximum(moving - 1, 0)), s)
            return carry

        few = moving <= 2
        lax.fori_loop(start, jnp.where(few & (moving > 0), end, start), pair_step, 0)
        lax.fori_loop(start, jnp.where(few, start, end), all_step, 0)

    planes = pl.pallas_call(
        middle_kernel,
        name="middle",
        compiler_params=GRANT,
        in_specs=[SMEM] * 2 + [VMEM] * 6,
        out_shape=pltpu.VMEM((mine, full, wide), jnp.float32),
        scratch_shapes=[pltpu.VMEM((2, full, wide), jnp.float32)],
    )(*in_smem(dirs, exts), *in_vmem(planes, parcel, far_parcel, near[1], far_side, taps))

    def late_kernel(
        dir_ref, ext_ref, albedo_ref, planes_ref, last_ref, far_last_ref, taps_ref,
        gain_near_ref, through_near_ref, gain_far_ref, through_far_ref, out_ref, plane, wall, lit,
    ):
        light = lax.axis_index("light")
        depth = lax.axis_index("depth")
        own_row = pl.multiple_of(depth * depth_len, BZ)
        other_row = pl.multiple_of((1 - depth) * depth_len, BZ)
        wall[pl.ds(own_row, depth_len), :] = last_ref[...]
        wall[pl.ds(other_row, depth_len), :] = far_last_ref[...]
        ups, rank, colour = sorted_colours(dir_ref, depth)
        inside = inside_lanes()
        ups_move = light % 2 == 1
        moving = jnp.where(ups_move, ups, mine - ups)
        first = jnp.where(ups_move, 0, ups)
        for i in range(mine):
            plane[i] = planes_ref[i]

        def advance(places):
            results = []
            for at in places:
                c = colour(at)
                before = planes_ref[at]
                after = blurred(before, wall[...], ext_ref[depth * mine + c], inside, taps_ref[c])
                moves = (at >= first) & (at < first + moving)
                results.append(jnp.where(moves, after, before))
            for at, after in zip(places, results):
                plane[at] = after

        @pl.when((moving > 0) & (moving <= 2))
        def _():
            advance((first, first + moving - 1))

        @pl.when(moving > 2)
        def _():
            advance(range(mine))

        in_front = depth == 0
        for i in range(mine):
            for half, row in enumerate((own_row, other_row)):
                lit[half, i] = plane[rank[i], pl.ds(row, depth_len), pl.ds(0, height_len)]
            shade = albedo_ref[depth * mine + i]
            sums = []
            for half, gain in enumerate((gain_near_ref, gain_far_ref)):
                parts = [None] * blocks
                for z in range(depth_len):
                    for j in range(blocks):
                        span = pl.ds(j * LANES, LANES)
                        part = lit[half, i, pl.ds(z, 1), span] * gain[i, z, :, span]
                        parts[j] = part if z == 0 else parts[j] + part
                sums.append(parts)
            for j in range(blocks):
                span = pl.ds(j * LANES, LANES)
                front = jnp.where(in_front, sums[0][j], sums[1][j])
                back = jnp.where(in_front, sums[1][j], sums[0][j])
                through = jnp.where(in_front, through_near_ref[:, span], through_far_ref[:, span])
                out_ref[i, :, span] = shade * (front + through * back)

    return pl.pallas_call(
        late_kernel,
        name="late",
        compiler_params=GRANT,
        in_specs=[SMEM] * 3 + [VMEM] * 8,
        out_specs=VMEM,
        out_shape=jax.ShapeDtypeStruct((mine, slices, height_len), jnp.float32),
        scratch_shapes=[
            pltpu.VMEM((mine, full, wide), jnp.float32),
            pltpu.VMEM((full, wide), jnp.float32),
            pltpu.VMEM((groups, mine, depth_len, height_len), jnp.float32),
        ],
    )(
        *in_smem(dirs, exts, albedos),
        *in_vmem(planes, near[0], far_last, taps),
        *in_vmem(gain_near, through_near, gain_far, through_far),
    )


def solution(mesh):
    in_specs = (
        P("light", "depth", "height"),
        P("depth", None),
        P(),
        P(None, "depth", "height"),
        P(),
        P(),
        P(),
    )
    out_specs = P("depth", "light", "height")

    return jax.shard_map(local, mesh=mesh, in_specs=in_specs, out_specs=out_specs, check_vma=False)
```
